32 devices in a mesh: ep: 8 (over z, y), tp: 4 (over x, core).
Axes of the slice: x: 2, y: 2, z: 4, core: 2. Of those that a mesh axis runs over, the one named last changes fastest.
Arguments:
- tokens: bfloat16 [3072, 2048], P('ep'), may hold values from -6 to 6
- first_gain: bfloat16 [2048], P('ep'), may hold values from 0.5 to 1.5
- query_weight: bfloat16 [2048, 2048], P('ep', 'tp'), may hold values from -0.125 to 0.125
- key_weight: bfloat16 [2048, 2048], P('ep', 'tp'), may hold values from -0.125 to 0.125
- value_weight: bfloat16 [2048, 2048], P('ep', 'tp'), may hold values from -0.125 to 0.125
- output_weight: bfloat16 [2048, 2048], P('tp', 'ep'), may hold values from -1.5 to 1.5
- second_gain: bfloat16 [2048], P('ep'), may hold values from 0.5 to 1.5
- shared_logit: bfloat16 [2048], P('ep'), may hold values from -0.125 to 0.125
- shared_gate: bfloat16 [2048, 5632], P('ep', 'tp'), may hold values from -0.125 to 0.125
- shared_up: bfloat16 [2048, 5632], P('ep', 'tp'), may hold values from -0.125 to 0.125
- shared_down: bfloat16 [5632, 2048], P('tp', 'ep'), may hold values from -0.078125 to 0.078125
- routed_gate_weight: bfloat16 [8, 2048, 1408], P('ep', None, 'tp'), may hold values from -0.125 to 0.125
- routed_up_weight: bfloat16 [8, 2048, 1408], P('ep', None, 'tp'), may hold values from -0.125 to 0.125
- expert_down: bfloat16 [8, 1408, 2048], P('ep', 'tp'), may hold values from -0.15625 to 0.15625
- route_ids: int32 [3072, 4], P('ep'), may hold values from 0 to 7, all different within a row; in each aligned block of 384 rows (0 to 383, 384 to 767, ...) at most 384 rows name the same one
- route_gates: float32 [3072, 4], P('ep'), may hold values from 0.15 to 0.4
- piece_start: int32 [8], P('ep'), may hold values from 0 to 256, as said below
- piece_length: int32 [8], P('ep'), may hold values from 128 to 256, as said below
- block_grad: bfloat16 [3072, 2048], P('ep'), may hold values from -6 to 6
Outputs:
- block_out: bfloat16 [3072, 2048], P('ep')
- tokens_grad: float32 [3072, 2048], P('ep')
- first_gain_grad: float32 [2048], P('ep')
- query_grad: float32 [2048, 2048], P('ep', 'tp')
- key_grad: float32 [2048, 2048], P('ep', 'tp')
- value_grad: float32 [2048, 2048], P('ep', 'tp')
- output_grad: float32 [2048, 2048], P('tp', 'ep')
- second_gain_grad: float32 [2048], P('ep')
- shared_logit_grad: float32 [2048], P('ep')
- shared_gate_grad: float32 [2048, 5632], P('ep', 'tp')
- shared_up_grad: float32 [2048, 5632], P('ep', 'tp')
- shared_down_grad: float32 [5632, 2048], P('tp', 'ep')
- expert_gate_grad: float32 [8, 2048, 1408], P('ep', None, 'tp')
- expert_up_grad: float32 [8, 2048, 1408], P('ep', None, 'tp')
- expert_down_grad: float32 [8, 1408, 2048], P('ep', 'tp')
- rms_values: float32 [8, 3], P('ep')
The draws below stay inside these ranges and needn't reach their ends.
Inputs may be any that keep to these rules, and one draw needn't show every extreme that they name: `route_ids`: each token names 4 different experts; among the 384 tokens of one sequence no expert is named by more than 384 tokens, and one expert by exactly 384. piece_start + piece_length <= 384 in every sequence. `piece_length`: some sequence has a piece of exactly 256 tokens.
All inputs are finite; a program needn't handle non-finite values.
Results may differ from the reference program's by a relative error of at most 0.014.
Values may be sent and summed in bfloat16 or wider, within the bound.
No kernel may reach another device: no remote copies, remote signals or barrier semaphores. Data moves between devices by JAX's collectives and lax.ppermute only.
A program may use at most 256 MiB of HBM per device.

```python
import math
import jax
import jax.numpy as jnp
import numpy as np
from jax import lax

D = 2048
HEADS = 16
HD = 128
FE = 1408
FS = 5632
TOP = 4
TOK_DEV = 384
PIECE = 256
EXPERTS = 8
CAP = 384
TOKENS = 3072
N_EP = 8
N_TP = 4


def piece_pair(key):
    base = jax.random.fold_in(key, 11)
    first, second, third = jax.random.split(base, 3)
    length = jax.random.randint(first, (N_EP,), PIECE // 2, PIECE + 1)
    chosen = jax.random.randint(second, (), 0, N_EP)
    indices = jnp.arange(N_EP)
    shortest = (chosen + 1) % N_EP
    earliest = (chosen + 2) % N_EP
    length = jnp.where(indices == chosen, PIECE, length)
    length = jnp.where(indices == shortest, PIECE // 2, length).astype(jnp.int32)
    start = jax.random.randint(third, (N_EP,), 0, TOK_DEV - length + 1)
    start = jnp.where(indices == shortest, TOK_DEV - PIECE // 2, start)
    start = jnp.where(indices == earliest, 0, start)
    return (start.astype(jnp.int32), length)


def draw_piece_start(key, part):
    return piece_pair(key)[0]


def draw_piece_length(key, part):
    return piece_pair(key)[1]


def levels(own_key, shape, shards, low, top_value):
    level = 1.0
    for position, shards_of in shards:
        steps = jax.random.uniform(jax.random.fold_in(jax.random.fold_in(own_key, 6), position), (shards_of,), jnp.float32, low / len(shards), top_value / len(shards))
        level = level * jnp.repeat(jnp.exp(steps), shape[position] // shards_of).reshape((-1,) + (1,) * (len(shape) - 1 - position))
    return level


def shared_out(key, own, number, rows, number_of, top, bound, slope):
    ranking = jax.random.permutation(key, number_of)
    heavy_load, usual = shares(number_of, rows * top, bound, slope, True), shares(number_of, rows * top, bound, slope, False)
    places = jnp.arange(number_of)

    def named(lengths, turn):
        used = int((lengths > 0).sum())
        fixed = max(1, used // 4)
        shifted = fixed + (places - fixed + turn * (used - fixed)) % max(1, number_of - fixed)
        return jnp.zeros((number_of,), jnp.int32).at[ranking[jnp.where(places < fixed, places, shifted)]].set(jnp.asarray(lengths, jnp.int32))

    lengths = jnp.where(number % 4 == 0, named(heavy_load, number // 4), named(usual, number - number // 4 - 1))
    mixed = jax.random.permutation(jax.random.fold_in(own, 3), number_of)
    donor, taker = mixed[0:number_of // 2 * 2:2], mixed[1:number_of // 2 * 2:2]
    margin = jnp.minimum(lengths[donor] - 1, bound - lengths[taker]) // 2
    margin = jnp.where((donor == ranking[0]) | (taker == ranking[0]) | (lengths[taker] == 0), 0, jnp.maximum(margin, 0))
    shifted = jax.random.randint(jax.random.fold_in(own, 4), (number_of // 2,), 0, 1 << 20) % (margin + 1)
    lengths = lengths.at[donor].add(-shifted).at[taker].add(shifted)
    members = jnp.searchsorted(jnp.cumsum(lengths), jnp.arange(rows * top), side="right").astype(jnp.int32)
    listing = members.reshape(top, rows).T
    listing = listing[jax.random.permutation(jax.random.fold_in(own, 1), rows)]
    turn = jax.random.randint(jax.random.fold_in(own, 2), (rows, 1), 0, top)
    return jnp.take_along_axis(listing, (jnp.arange(top)[None, :] + turn) % top, axis=1)


def shares(amount, total, most, slope, full):
    portions = [(1 << 20) // math.isqrt(rank ** slope) + 1 for rank in range(1, amount + 1)]
    largest = most if full else min(most, max(-(-total // amount), total * portions[0] // sum(portions)))
    least = 1 if total - largest >= amount - 1 else 0
    given, spare = [largest] + [least] * (amount - 1), total - largest - least * (amount - 1)
    while spare > 0:
        movable = [i for i in range(1, amount) if given[i] < largest] or [i for i in range(1, amount) if given[i] < most]
        pool, left = sum([portions[i] for i in movable]), spare
        for i in movable:
            addition = min(most - given[i], max(1, left * portions[i] // pool), spare)
            given[i] = given[i] + addition
            spare = spare - addition
    return np.array(given)


def noise(stream_key, extent, spread, bound, pieces=(), held_as=jnp.bfloat16):
    values = jax.random.normal(stream_key, extent, jnp.float32) * spread
    if len(pieces) > 0:
        values = levels(stream_key, extent, pieces, -0.22, 0.18) * values
    return jnp.clip(values, min=-bound, max=bound).astype(held_as)


def setup_inputs(seed: int = 0) -> dict:
    key_list = jax.random.split(jax.random.key(seed), 20)
    tokens = noise(key_list[0], (TOKENS, D), 1.0, 6.0, ((0, 8),))
    first_gain = jnp.clip(1.0 + 0.1 * jax.random.normal(key_list[1], (D,), jnp.float32), 0.5, 1.5).astype(jnp.bfloat16)
    query_weight = noise(key_list[2], (D, HEADS * HD), D ** -0.5, 0.125, ((0, 8), (1, 4)))
    key_weight = noise(key_list[3], (D, HEADS * HD), D ** -0.5, 0.125, ((0, 8), (1, 4)))
    value_weight = noise(key_list[4], (D, HEADS * HD), D ** -0.5, 0.125, ((0, 8), (1, 4)))
    output_weight = noise(key_list[5], (HEADS * HD, D), (max(HEADS * HD // 128, 4)) ** -0.5, 1.5, ((0, 4), (1, 8)))
    second_gain = jnp.clip(1.0 + 0.1 * jax.random.normal(key_list[6], (D,), jnp.float32), 0.5, 1.5).astype(jnp.bfloat16)
    shared_logit = noise(key_list[7], (D,), D ** -0.5, 0.125, ((0, 8),))
    shared_gate = noise(key_list[8], (D, FS), D ** -0.5, 0.125, ((0, 8), (1, 4)))
    shared_up = noise(key_list[9], (D, FS), D ** -0.5, 0.125, ((0, 8), (1, 4)))
    shared_down = noise(key_list[10], (FS, D), FS ** -0.5, 0.078125, ((0, 4), (1, 8)))
    routed_gate_weight = noise(key_list[11], (EXPERTS, D, FE), D ** -0.5, 0.125, ((0, 8), (2, 4)))
    routed_up_weight = noise(key_list[12], (EXPERTS, D, FE), D ** -0.5, 0.125, ((0, 8), (2, 4)))
    expert_down = noise(key_list[13], (EXPERTS, FE, D), FE ** -0.5, 0.15625, ((0, 8), (1, 4)))
    route_ids_keys = jax.random.split(jax.random.fold_in(key_list[14], 1), TOKENS // TOK_DEV)
    route_ids_turns = jax.random.permutation(jax.random.fold_in(key_list[14], 3), TOKENS // TOK_DEV)
    route_ids = jax.vmap(lambda own, number: shared_out(jax.random.fold_in(key_list[14], 2), own, number, TOK_DEV, EXPERTS, TOP, CAP, 2))(route_ids_keys, route_ids_turns).reshape((TOKENS, TOP))
    route_gates = jnp.clip(0.15 + 0.25 * jax.random.uniform(key_list[15], (TOKENS, TOP), jnp.float32) ** levels(key_list[15], (TOKENS, TOP), ((0, 8),), -0.2, 0.2), 0.15, 0.4)
    piece_start = draw_piece_start(jax.random.fold_in(key_list[19], 71), 0)
    piece_length = draw_piece_length(jax.random.fold_in(key_list[19], 71), 0)
    block_grad = noise(key_list[18], (TOKENS, D), 1.0, 6.0, ((0, 8),))
    return dict(tokens=tokens, first_gain=first_gain, query_weight=query_weight, key_weight=key_weight, value_weight=value_weight, output_weight=output_weight, second_gain=second_gain, shared_logit=shared_logit, shared_gate=shared_gate, shared_up=shared_up, shared_down=shared_down, routed_gate_weight=routed_gate_weight, routed_up_weight=routed_up_weight, expert_down=expert_down, route_ids=route_ids, route_gates=route_gates, piece_start=piece_start, piece_length=piece_length, block_grad=block_grad)


@jax.custom_vjp
def reduced_value(v):
    return lax.optimization_barrier(v.astype(jnp.bfloat16)).astype(jnp.float32)

@jax.custom_vjp
def reduced_gradient(v):
    return v

def low_keep(v):
    return (reduced_value(v), None)

def low_pass(kept, grad):
    return (grad,)

def back_keep(v):
    return (v, None)

def back_low(kept, grad):
    return (reduced_value(grad),)
reduced_value.defvjp(low_keep, low_pass)
reduced_gradient.defvjp(back_keep, back_low)
HIGHEST_DIGITS = lax.Precision.HIGHEST
EPS = 1e-06

def matrix_product(left, right):
    return jnp.dot(left, right, precision=HIGHEST_DIGITS, preferred_element_type=jnp.float32)

def rms_scale(values):
    return lax.rsqrt(lax.optimization_barrier(jnp.mean(values * values, axis=-1, keepdims=True)) + EPS)

def slot_index(route_rows, experts, capacity):
    count, chosen_count = route_rows.shape
    chosen = route_rows.reshape(count * chosen_count)
    onehot = (chosen[:, None] == jnp.arange(experts, dtype=jnp.int32)[None, :]).astype(jnp.int32)
    earlier = jnp.cumsum(onehot, axis=0) - onehot
    placed = lax.optimization_barrier(jnp.sum(earlier * onehot, axis=1))
    return (chosen * capacity + placed).astype(jnp.int32)

def attend(block):
    query, key, value, start, length = block
    positions = jnp.arange(TOK_DEV, dtype=jnp.int32)
    inside = (positions >= start) & (positions < start + length)
    visible = (positions[None, :] <= positions[:, None]) | inside[:, None] & inside[None, :]
    scores = jnp.einsum('qhd,khd->hqk', query, key, precision=HIGHEST_DIGITS) * HD ** (-0.5)
    scores = reduced_gradient(scores)
    scores = jnp.where(visible[None], scores, -1e+30)
    probs = jax.nn.softmax(scores, axis=-1)
    return jnp.einsum('hqk,khd->qhd', reduced_value(probs), value, precision=HIGHEST_DIGITS)

def forward(tokens, first_gain, query_weight, key_weight, value_weight, output_weight, second_gain, shared_logit, shared_gate, shared_up, shared_down, routed_gate_weight, routed_up_weight, expert_down, route_ids, route_gates, piece_start, piece_length):
    act1 = reduced_value(tokens * rms_scale(tokens) * first_gain)

    def project(weight):
        return reduced_gradient(reduced_value(matrix_product(act1, weight))).reshape(N_EP, TOK_DEV, HEADS, HD)
    query = project(query_weight)
    key = project(key_weight)
    value = project(value_weight)
    mixed = lax.map(jax.checkpoint(attend), (query, key, value, piece_start, piece_length))
    attn_mix = reduced_gradient(reduced_value(mixed.reshape(TOKENS, HEADS * HD)))
    attn_branch = reduced_gradient(matrix_product(attn_mix, output_weight))
    resid = tokens + attn_branch
    act2 = reduced_value(resid * rms_scale(resid) * second_gain)
    shared_score = jax.nn.sigmoid(matrix_product(act2, shared_logit))
    sgate = reduced_gradient(matrix_product(act2, shared_gate))
    sup = reduced_gradient(matrix_product(act2, shared_up))
    shidden = reduced_value(jax.nn.silu(sgate) * sup)
    shared_branch = reduced_gradient(matrix_product(shidden, shared_down))
    local_slots = jax.vmap(lambda token_rows: slot_index(token_rows, EXPERTS, CAP))(route_ids.reshape(N_EP, TOK_DEV, TOP))
    expert_of = local_slots // CAP
    placed = local_slots % CAP
    sequence = jnp.arange(N_EP, dtype=jnp.int32)[:, None]
    global_slot = (expert_of * (N_EP * CAP) + sequence * CAP + placed).reshape(TOKENS * TOP).astype(jnp.int32)
    pair_rows = jnp.repeat(act2, TOP, axis=0)
    expert_rows = jnp.zeros((EXPERTS * N_EP * CAP, D), jnp.float32).at[global_slot].set(pair_rows)
    expert_rows = expert_rows.reshape(EXPERTS, N_EP * CAP, D)
    block_width = FE // N_TP
    combined = jnp.zeros((EXPERTS, N_EP * CAP, D), jnp.float32)
    for block in range(N_TP):
        lower_bound_value = block * block_width
        upper_bound_value = lower_bound_value + block_width
        token_rows_duplicate = reduced_gradient(expert_rows)
        expert_gate_product = reduced_gradient(jnp.einsum('npb,nbc->npc', token_rows_duplicate, routed_gate_weight[:, :, lower_bound_value:upper_bound_value], precision=HIGHEST_DIGITS))
        expert_up_product = reduced_gradient(jnp.einsum('npb,nbc->npc', token_rows_duplicate, routed_up_weight[:, :, lower_bound_value:upper_bound_value], precision=HIGHEST_DIGITS))
        expert_hidden_state = reduced_value(jax.nn.silu(expert_gate_product) * expert_up_product)
        epart = reduced_gradient(reduced_value(jnp.einsum('erf,efd->erd', expert_hidden_state, expert_down[:, lower_bound_value:upper_bound_value, :], precision=HIGHEST_DIGITS)))
        combined = combined + epart
    picked = combined.reshape(EXPERTS * N_EP * CAP, D)[global_slot].reshape(TOKENS, TOP, D)
    routed = lax.optimization_barrier(jnp.sum(route_gates[:, :, None] * picked, axis=1))
    ffn_branch = routed + shared_score[:, None] * shared_branch
    return (resid + ffn_branch, attn_branch, ffn_branch)

def sequence_rms(values):
    grouped = values.reshape(N_EP, TOK_DEV * D)
    return jnp.sqrt(lax.optimization_barrier(jnp.mean(grouped * grouped, axis=1)))

def reference(tokens, first_gain, query_weight, key_weight, value_weight, output_weight, second_gain, shared_logit, shared_gate, shared_up, shared_down, routed_gate_weight, routed_up_weight, expert_down, route_ids, route_gates, piece_start, piece_length, block_grad):
    floats = tuple((array.astype(jnp.float32) for array in (tokens, first_gain, query_weight, key_weight, value_weight, output_weight, second_gain, shared_logit, shared_gate, shared_up, shared_down, routed_gate_weight, routed_up_weight, expert_down)))
    gates32 = route_gates.astype(jnp.float32)

    def closed(*params):
        return forward(*params, route_ids, gates32, piece_start, piece_length)
    outputs, pull = jax.vjp(closed, *floats)
    block_out, attn_branch, ffn_branch = outputs
    grads = pull((block_grad.astype(jnp.float32), jnp.zeros_like(attn_branch), jnp.zeros_like(ffn_branch)))
    rms_values = jnp.stack([sequence_rms(attn_branch), sequence_rms(ffn_branch), sequence_rms(block_out)], axis=1)
    return (block_out.astype(jnp.bfloat16), grads[0], grads[1], grads[2], grads[3], grads[4], grads[5], grads[6], grads[7], grads[8], grads[9], grads[10], grads[11], grads[12], grads[13], rms_values)
```

```python
import jax
import jax.numpy as jnp
from jax import lax
from jax.sharding import PartitionSpec as P

HD = 128
EPS = 1e-06
BF = jnp.bfloat16
F32 = jnp.float32


def nn(left, right):
    return lax.dot_general(left, right, (((1,), (0,)), ((), ())), preferred_element_type=F32)


def nt(left, right):
    return lax.dot_general(left, right, (((1,), (1,)), ((), ())), preferred_element_type=F32)


def tn(left, right):
    return lax.dot_general(left, right, (((0,), (0,)), ((), ())), preferred_element_type=F32)


def at(array, index):
    return lax.dynamic_index_in_dim(array, index, 0, keepdims=False)


def put(array, value, index):
    return lax.dynamic_update_index_in_dim(array, value, index, 0)


def swap_inner(value):
    size = lax.axis_size("ep")
    return lax.ppermute(value, "ep", [(i, i ^ 1) for i in range(size)])


def ring_outer(value):
    size = lax.axis_size("ep")
    return lax.ppermute(value, "ep", [(i, (i + 2) % size) for i in range(size)])


def swap_tp(value, mask):
    size = lax.axis_size("tp")
    return lax.ppermute(value, "tp", [(i, i ^ mask) for i in range(size)])


def gather_ep(shard):
    size = lax.axis_size("ep")
    rounds = size // 2
    me = lax.axis_index("ep")
    outer, inner = me // 2, me % 2
    whole = jnp.zeros((size,) + shard.shape, shard.dtype)
    current = shard
    for k in range(rounds):
        where = (outer + rounds - k) % rounds * 2
        other = swap_inner(current)
        whole = put(whole, current, where + inner)
        following = ring_outer(current) if k < rounds - 1 else None
        whole = put(whole, other, where + 1 - inner)
        current = following
    return whole


def scatter_ep(parts, sent=BF):
    size = lax.axis_size("ep")
    rounds = size // 2
    me = lax.axis_index("ep")
    outer, inner = me // 2, me % 2
    arrived = None
    for k in list(range(1, rounds)) + [0]:
        where = (outer + rounds - k) % rounds * 2
        other = swap_inner(at(parts, where + 1 - inner).astype(sent))
        total = at(parts, where + inner).astype(F32) + other.astype(F32)
        if arrived is not None:
            total = total + arrived.astype(F32)
        if k:
            arrived = ring_outer(total.astype(sent))
    return total


def gather_tp(shard):
    me = lax.axis_index("tp")
    whole = jnp.zeros((lax.axis_size("tp"),) + shard.shape, shard.dtype)
    far = swap_tp(shard, 2)
    whole = put(whole, shard, me)
    whole = put(whole, swap_tp(shard, 1), me ^ 1)
    whole = put(whole, far, me ^ 2)
    return put(whole, swap_tp(far, 1), me ^ 3)


def scatter_tp(parts, sent=BF):
    me = lax.axis_index("tp")
    near_far = swap_tp(at(parts, me ^ 3).astype(sent), 1)
    far = at(parts, me ^ 2).astype(F32) + near_far.astype(F32)
    far = swap_tp(far.astype(sent), 2)
    near = swap_tp(at(parts, me ^ 1).astype(sent), 1)
    return at(parts, me).astype(F32) + near.astype(F32) + far.astype(F32)


def sum_tp(value):
    value = value + swap_tp(value, 1)
    return value + swap_tp(value, 2)


def rms_scale(values):
    return lax.rsqrt(jnp.mean(values * values, axis=-1, keepdims=True) + EPS)


def norm_back(grad, values, scale, gain):
    weighted = grad * gain
    inner = jnp.mean(values * weighted, axis=-1, keepdims=True)
    return (scale * weighted - values * scale**3 * inner, jnp.sum(grad * values * scale, axis=0))


def gated_back(grad_hidden, gate_val, up_val):
    squash = jax.nn.sigmoid(gate_val)
    grad_gate = grad_hidden * up_val * squash * (1.0 + gate_val * (1.0 - squash))
    grad_up = grad_hidden * gate_val * squash
    return (grad_gate.astype(BF), grad_up.astype(BF))


def expert_step(act, gout, gates, logit32, routed, shared):
    r_gate, r_up, r_down = routed
    s_gate, s_up, s_down = shared
    score = jax.nn.sigmoid(jnp.sum(act.astype(F32) * logit32, axis=1, keepdims=True))
    r_gate_val, r_up_val = nt(act, r_gate), nt(act, r_up)
    s_gate_val, s_up_val = nt(act, s_gate), nt(act, s_up)
    r_hidden = (jax.nn.silu(r_gate_val) * r_up_val * gates).astype(BF)
    s_plain = jax.nn.silu(s_gate_val) * s_up_val
    s_hidden = (s_plain * score).astype(BF)
    out = (nn(r_hidden, r_down) + nn(s_hidden, s_down)).astype(BF)
    r_back = nt(gout, r_down)
    s_back = nt(gout, s_down)
    r_dgate, r_dup = gated_back(r_back * gates, r_gate_val, r_up_val)
    s_dgate, s_dup = gated_back(s_back * score, s_gate_val, s_up_val)
    gscore = score * (1.0 - score) * jnp.sum(s_plain * s_back, axis=1, keepdims=True)
    gact = nn(r_dgate, r_gate) + nn(r_dup, r_up) + nn(s_dgate, s_gate) + nn(s_dup, s_up)
    gact = (gact + gscore * logit32).astype(BF)
    logit_part = jnp.sum(act.astype(F32) * gscore, axis=0)
    pairs = (
        (r_dgate, act),
        (r_dup, act),
        (r_hidden, gout),
        (s_dgate, act),
        (s_dup, act),
        (s_hidden, gout),
    )
    return out, gact, (logit_part,) + tuple(tn(left, right) for left, right in pairs)


def experts(act, gout, gates, logit32, routed, shared, most=1024):
    rows, width = act.shape
    steps = -(-rows // most)
    if steps == 1:
        out, gact, sums = expert_step(act, gout, gates, logit32, routed, shared)
        return out, gact, sums[0], sums[1:]

    def step(totals, block):
        out, gact, sums = expert_step(*block, logit32, routed, shared)
        return tuple(t + s for t, s in zip(totals, sums)), (out, gact)

    blocks = tuple(x.reshape(steps, rows // steps, -1) for x in (act, gout, gates))
    sizes = [(width,)] + [w.shape for w in routed + shared]
    totals = tuple(jnp.zeros(size, F32) for size in sizes)
    sums, (out, gact) = lax.scan(step, totals, blocks)
    return out.reshape(rows, width), gact.reshape(rows, width), sums[0], sums[1:]


def columns(array, head):
    return array[:, head * HD : (head + 1) * HD]


def on_device(
    tokens,
    first_gain,
    query_weight,
    key_weight,
    value_weight,
    output_weight,
    second_gain,
    shared_logit,
    shared_gate,
    shared_up,
    shared_down,
    routed_gate_weight,
    routed_up_weight,
    expert_down,
    route_ids,
    route_gates,
    piece_start,
    piece_length,
    block_grad,
):
    groups = lax.axis_size("ep")
    quarters = lax.axis_size("tp")
    me_ep = lax.axis_index("ep")
    me_tp = lax.axis_index("tp")
    count, width = tokens.shape
    part = count // quarters
    local_heads = query_weight.shape[1] // HD
    wide = local_heads * HD
    factor = HD ** (-0.5)

    def own(array):
        return lax.dynamic_slice_in_dim(array, me_tp * part, part, 0)

    vectors = jnp.stack([first_gain, second_gain, shared_logit])
    vectors = gather_ep(jnp.pad(vectors, ((0, 5), (0, 0))))
    vectors = vectors.transpose(1, 0, 2).reshape(8, width)
    gain_one32 = vectors[0:1].astype(F32)
    gain_two32 = vectors[1:2].astype(F32)
    logit32 = vectors[2:3].astype(F32)
    w_qkv = gather_ep(jnp.concatenate([query_weight, key_weight, value_weight], axis=1))
    w_qkv = w_qkv.reshape(width, 3 * wide)
    w_out = gather_ep(output_weight.T).reshape(width, wide)

    def units_first(array):
        return gather_tp(array).reshape(-1, width)

    r_gate = units_first(routed_gate_weight[0].T)
    r_up = units_first(routed_up_weight[0].T)
    r_down = units_first(expert_down[0])

    units = shared_down.shape[0]
    piece = units // groups
    shared = jnp.stack([shared_gate.T, shared_up.T, shared_down]).reshape(3, groups, piece, -1)
    shared = lax.all_to_all(shared, "ep", split_axis=1, concat_axis=1, tiled=True)
    shared = shared.transpose(0, 2, 1, 3).reshape(3, piece, width)
    shared = gather_tp(shared)
    shared = shared.transpose(1, 0, 2, 3).reshape(3, quarters * piece, width)
    s_gate, s_up, s_down = shared[0], shared[1], shared[2]

    inputs32 = tokens.astype(F32)
    scale_one = rms_scale(inputs32)
    act1 = (inputs32 * scale_one * gain_one32).astype(BF)
    qkv = nn(act1, w_qkv).astype(BF)
    query, key, value = qkv[:, :wide], qkv[:, wide : 2 * wide], qkv[:, 2 * wide :]
    positions = jnp.arange(count, dtype=jnp.int32)
    start = piece_start[0]
    inside = (positions >= start) & (positions < start + piece_length[0])
    visible = (positions[None, :] <= positions[:, None]) | inside[:, None] & inside[None, :]
    all_lse, mixes = [], []
    for h in range(local_heads):
        scores = jnp.where(visible, nt(columns(query, h), columns(key, h)) * factor, -1e30)
        highest = jnp.max(scores, axis=-1, keepdims=True)
        lse = highest + jnp.log(jnp.sum(jnp.exp(scores - highest), axis=-1, keepdims=True))
        probs = jnp.exp(scores - lse).astype(BF)
        all_lse.append(lse)
        mixes.append(nn(probs, columns(value, h)).astype(BF))
    attn_mix = jnp.concatenate(mixes, axis=1)
    branch = nt(attn_mix, w_out).reshape(quarters, part, width)
    attn_branch = scatter_tp(branch, F32)

    inputs_own = own(tokens).astype(F32)
    resid = inputs_own + attn_branch
    scale_two = rms_scale(resid)
    act2 = (resid * scale_two * gain_two32).astype(BF)

    dense = jnp.sum(
        own(route_gates)[:, :, None]
        * (own(route_ids)[:, :, None] == jnp.arange(groups, dtype=jnp.int32)).astype(F32),
        axis=1,
    )
    gates = gather_ep(dense).reshape(groups * part, groups)
    gates = jnp.sum(
        jnp.where(jnp.arange(groups)[None, :] == me_ep, gates, 0.0), axis=1, keepdims=True
    )
    gout_all = gather_ep(own(block_grad)).reshape(groups * part, width)
    act_all = gather_ep(act2).reshape(groups * part, width)

    ffn_part, gact_part, logit_part, sums = experts(
        act_all, gout_all, gates, logit32, (r_gate, r_up, r_down), (s_gate, s_up, s_down)
    )
    ffn_branch = scatter_ep(ffn_part.reshape(groups, part, width))
    block_sum = resid + ffn_branch
    block_out = gather_tp(block_sum.astype(BF)).reshape(count, width)
    squares = jnp.stack(
        [
            jnp.sum(attn_branch * attn_branch),
            jnp.sum(ffn_branch * ffn_branch),
            jnp.sum(block_sum * block_sum),
        ]
    )
    rms_values = jnp.sqrt(sum_tp(squares) / (count * width))[None, :]

    gact2 = scatter_ep(gact_part.reshape(groups, part, width))
    sums = [scatter_tp(total.astype(BF).reshape(quarters, -1, width)) for total in sums]
    gate_grad, up_grad, down_grad = sums[0].T, sums[1].T, sums[2]
    shared_grads = jnp.stack(sums[3:])
    shared_grads = shared_grads.astype(BF).reshape(3, piece, groups, -1).transpose(0, 2, 1, 3)
    shared_grads = lax.all_to_all(shared_grads, "ep", split_axis=1, concat_axis=1, tiled=True)
    shared_grads = shared_grads.reshape(3, units, -1)
    sgate_grad = shared_grads[0].T.astype(F32)
    sup_grad = shared_grads[1].T.astype(F32)
    sdown_grad = shared_grads[2].astype(F32)

    resid_part, gain_two_part = norm_back(gact2, resid, scale_two, gain_two32)
    gresid = own(block_grad).astype(F32) + resid_part
    gattn = gather_tp(gresid.astype(BF)).reshape(count, width)
    output_grad = scatter_ep(tn(gattn, attn_mix).astype(BF).reshape(groups, -1, wide)).T
    gmix = nn(gattn, w_out).astype(BF)
    gqs, gks, gvs = [], [], []
    for h in range(local_heads):
        query_h, key_h, gmix_h = columns(query, h), columns(key, h), columns(gmix, h)
        scores = jnp.where(visible, nt(query_h, key_h) * factor, -1e30)
        probs = jnp.exp(scores - all_lse[h])
        gprob = nt(gmix_h, columns(value, h))
        gvs.append(tn(probs.astype(BF), gmix_h).astype(BF))
        inner = jnp.sum(probs * gprob, axis=-1, keepdims=True)
        gscores = (probs * (gprob - inner)).astype(BF)
        gqs.append((nn(gscores, key_h) * factor).astype(BF))
        gks.append((tn(gscores, query_h) * factor).astype(BF))
    gqkv = jnp.concatenate(gqs + gks + gvs, axis=1)
    qkv_grad = scatter_ep(tn(act1, gqkv).astype(BF).reshape(groups, -1, 3 * wide))
    gact1 = scatter_tp(nt(gqkv, w_qkv).astype(BF).reshape(quarters, part, width))
    input_part, gain_one_part = norm_back(gact1, inputs_own, own(scale_one), gain_one32)
    tokens_grad = gather_tp((gresid + input_part).astype(BF)).reshape(count, width).astype(F32)

    def summed(vector_parts):
        stacked = jnp.stack(vector_parts).reshape(len(vector_parts), groups, -1)
        return sum_tp(scatter_ep(stacked.transpose(1, 0, 2), F32))

    early = summed([gain_two_part, logit_part])
    late = summed([gain_one_part])
    return (
        block_out,
        tokens_grad,
        late[0],
        qkv_grad[:, :wide],
        qkv_grad[:, wide : 2 * wide],
        qkv_grad[:, 2 * wide :],
        output_grad,
        early[0],
        early[1],
        sgate_grad,
        sup_grad,
        sdown_grad,
        gate_grad[None],
        up_grad[None],
        down_grad[None],
        rms_values,
    )


def solution(mesh):
    in_specs = (
        P("ep", None),
        P("ep"),
        P("ep", "tp"),
        P("ep", "tp"),
        P("ep", "tp"),
        P("tp", "ep"),
        P("ep"),
        P("ep"),
        P("ep", "tp"),
        P("ep", "tp"),
        P("tp", "ep"),
        P("ep", None, "tp"),
        P("ep", None, "tp"),
        P("ep", "tp", None),
        P("ep", None),
        P("ep", None),
        P("ep"),
        P("ep"),
        P("ep", None),
    )
    out_specs = (
        P("ep", None),
        P("ep", None),
        P("ep"),
        P("ep", "tp"),
        P("ep", "tp"),
        P("ep", "tp"),
        P("tp", "ep"),
        P("ep"),
        P("ep"),
        P("ep", "tp"),
        P("ep", "tp"),
        P("tp", "ep"),
        P("ep", None, "tp"),
        P("ep", None, "tp"),
        P("ep", "tp", None),
        P("ep", None),
    )
    return jax.shard_map(
        on_device, mesh=mesh, in_specs=in_specs, out_specs=out_specs, check_vma=False
    )
```

```python
import jax
import jax.numpy as jnp
from jax import lax
from jax.sharding import PartitionSpec as P

HD = 128
EPS = 1e-06
BF = jnp.bfloat16
F32 = jnp.float32


def nn(left, right):
    return lax.dot_general(left, right, (((1,), (0,)), ((), ())), preferred_element_type=F32)


def nt(left, right):
    return lax.dot_general(left, right, (((1,), (1,)), ((), ())), preferred_element_type=F32)


def tn(left, right):
    return lax.dot_general(left, right, (((0,), (0,)), ((), ())), preferred_element_type=F32)


def at(array, index):
    return lax.dynamic_index_in_dim(array, index, 0, keepdims=False)


def put(array, value, index):
    return lax.dynamic_update_index_in_dim(array, value, index, 0)


def after(value, *earlier):
    return lax.optimization_barrier((value,) + earlier)[0]


def swap_inner(value):
    size = lax.axis_size("ep")
    return lax.ppermute(value, "ep", [(i, i ^ 1) for i in range(size)])


def ring_outer(value):
    size = lax.axis_size("ep")
    return lax.ppermute(value, "ep", [(i, (i + 2) % size) for i in range(size)])


def swap_tp(value, mask):
    size = lax.axis_size("tp")
    return lax.ppermute(value, "tp", [(i, i ^ mask) for i in range(size)])


def relative_to_absolute():
    size = lax.axis_size("ep")
    me = lax.axis_index("ep")
    outer, inner = me // 2, me % 2
    rounds = size // 2
    return [(outer + rounds - r // 2) % rounds * 2 + (inner ^ r % 2) for r in range(size)]


def gather_ep(shard):
    rounds = lax.axis_size("ep") // 2
    blocks = []
    current = shard
    for k in range(rounds):
        blocks += [current, swap_inner(current)]
        if k < rounds - 1:
            current = ring_outer(current)
    return blocks, current


def stack_static(blocks):
    whole = jnp.zeros((len(blocks),) + blocks[0].shape, blocks[0].dtype)
    for i, block in enumerate(blocks):
        whole = whole.at[i].set(block)
    return whole


def stack_absolute(blocks):
    whole = jnp.zeros((len(blocks),) + blocks[0].shape, blocks[0].dtype)
    for block, index in zip(blocks, relative_to_absolute()):
        whole = put(whole, block, index)
    return whole


def scatter_ep(block_of):
    rounds = lax.axis_size("ep") // 2
    arrived = other = None
    for k in list(range(1, rounds)) + [0]:
        away = block_of(2 * k + 1).astype(BF)
        if other is not None:
            away = after(away, other)
        other = swap_inner(away)
        total = block_of(2 * k).astype(F32) + other.astype(F32)
        if arrived is not None:
            total = total + arrived.astype(F32)
        if k:
            arrived = ring_outer(total.astype(BF))
    return total


def scatter_absolute(parts):
    order = relative_to_absolute()
    return scatter_ep(lambda r: at(parts, order[r]))


def gather_tp(shard):
    far = swap_tp(shard, 2)
    return [shard, swap_tp(shard, 1), far, swap_tp(far, 1)]


def gather_tp_rows(shard):
    me = lax.axis_index("tp")
    whole = jnp.zeros((lax.axis_size("tp"),) + shard.shape, shard.dtype)
    for j, block in enumerate(gather_tp(shard)):
        whole = put(whole, block, me ^ j)
    return whole.reshape(-1, shard.shape[-1])


def scatter_tp(block_of):
    near_far = swap_tp(block_of(3).astype(BF), 1)
    far = block_of(2).astype(F32) + near_far.astype(F32)
    near = swap_tp(block_of(1).astype(BF), 1)
    far = swap_tp(far.astype(BF), 2)
    return block_of(0).astype(F32) + near.astype(F32) + far.astype(F32)


def scatter_tp_rows(parts):
    me = lax.axis_index("tp")
    return scatter_tp(lambda j: at(parts, me ^ j))


def sum_tp(value):
    value = value + swap_tp(value, 1)
    return value + swap_tp(value, 2)


def rms_scale(values):
    return lax.rsqrt(jnp.mean(values * values, axis=-1, keepdims=True) + EPS)


def norm_back(grad, values, scale, gain):
    weighted = grad * gain
    inner = jnp.mean(values * weighted, axis=-1, keepdims=True)
    return (scale * weighted - values * scale**3 * inner, jnp.sum(grad * values * scale, axis=0))


def gated_back(grad_hidden, gate_val, up_val):
    squash = jax.nn.sigmoid(gate_val)
    grad_gate = grad_hidden * up_val * squash * (1.0 + gate_val * (1.0 - squash))
    grad_up = grad_hidden * gate_val * squash
    return (grad_gate.astype(BF), grad_up.astype(BF))


def expert_step(act, gout, gates, logit32, routed, shared):
    r_gate, r_up, r_down = routed
    s_gate, s_up, s_down = shared
    score = jax.nn.sigmoid(jnp.sum(act.astype(F32) * logit32, axis=1, keepdims=True))
    r_gate_val, r_up_val = nt(act, r_gate), nt(act, r_up)
    s_gate_val, s_up_val = nt(act, s_gate), nt(act, s_up)
    r_hidden = (jax.nn.silu(r_gate_val) * r_up_val * gates).astype(BF)
    s_plain = jax.nn.silu(s_gate_val) * s_up_val
    s_hidden = (s_plain * score).astype(BF)
    r_back = nt(gout, r_down)
    s_back = nt(gout, s_down)
    r_dgate, r_dup = gated_back(r_back * gates, r_gate_val, r_up_val)
    s_dgate, s_dup = gated_back(s_back * score, s_gate_val, s_up_val)
    gscore = score * (1.0 - score) * jnp.sum(s_plain * s_back, axis=1, keepdims=True)
    gact = nn(r_dgate, r_gate) + nn(r_dup, r_up) + nn(s_dgate, s_gate) + nn(s_dup, s_up)
    gact = (gact + gscore * logit32).astype(BF)
    act, gout, r_hidden, s_hidden, gscore = lax.optimization_barrier(
        (act, gout, r_hidden, s_hidden, gscore, gact)
    )[:5]
    logit_part = jnp.sum(act.astype(F32) * gscore, axis=0)
    pairs = (
        (r_dgate, act),
        (r_dup, act),
        (r_hidden, gout),
        (s_dgate, act),
        (s_dup, act),
        (s_hidden, gout),
    )
    out = (nn(r_hidden, r_down) + nn(s_hidden, s_down)).astype(BF)
    return out, gact, (logit_part,) + tuple(tn(left, right) for left, right in pairs)


def experts(act, gout, gates, logit32, routed, shared, most=1024):
    rows, width = act.shape
    steps = -(-rows // most)
    if steps == 1:
        out, gact, sums = expert_step(act, gout, gates, logit32, routed, shared)
        return out, gact, sums[0], sums[1:]

    def step(totals, block):
        out, gact, sums = expert_step(*block, logit32, routed, shared)
        return tuple(t + s for t, s in zip(totals, sums)), (out, gact)

    blocks = tuple(x.reshape(steps, rows // steps, -1) for x in (act, gout, gates))
    sizes = [(width,)] + [w.shape for w in routed + shared]
    totals = tuple(jnp.zeros(size, F32) for size in sizes)
    sums, (out, gact) = lax.scan(step, totals, blocks)
    return out.reshape(rows, width), gact.reshape(rows, width), sums[0], sums[1:]


def columns(array, head):
    return array[:, head * HD : (head + 1) * HD]


def on_device(
    tokens,
    first_gain,
    query_weight,
    key_weight,
    value_weight,
    output_weight,
    second_gain,
    shared_logit,
    shared_gate,
    shared_up,
    shared_down,
    routed_gate_weight,
    routed_up_weight,
    expert_down,
    route_ids,
    route_gates,
    piece_start,
    piece_length,
    block_grad,
):
    groups = lax.axis_size("ep")
    quarters = lax.axis_size("tp")
    me_ep = lax.axis_index("ep")
    me_tp = lax.axis_index("tp")
    count, width = tokens.shape
    part = count // quarters
    local_heads = query_weight.shape[1] // HD
    wide = local_heads * HD
    factor = HD ** (-0.5)

    def own(array):
        return lax.dynamic_slice_in_dim(array, me_tp * part, part, 0)

    dense = jnp.sum(
        own(route_gates)[:, :, None]
        * (own(route_ids)[:, :, None] == jnp.arange(groups, dtype=jnp.int32)).astype(F32),
        axis=1,
    )
    rows = query_weight.shape[0]
    high = dense.astype(BF)
    low = (dense - high.astype(F32)).astype(BF)
    packed = jnp.concatenate([high.reshape(-1), low.reshape(-1)]).reshape(-1, rows)
    spare = jnp.concatenate([jnp.stack([first_gain, second_gain, shared_logit]), packed]).T
    spare = jnp.pad(spare, ((0, 0), (0, -spare.shape[1] % 128)))
    blocks, last = gather_ep(
        jnp.concatenate([query_weight, key_weight, value_weight, spare], axis=1)
    )
    w_qkv = stack_absolute(blocks)
    spare = w_qkv[:, :, 3 * wide :]
    w_qkv = w_qkv.reshape(width, -1)
    vectors = spare[:, :, :3].reshape(width, 3).T.astype(F32)
    gain_one32, gain_two32, logit32 = vectors[0:1], vectors[1:2], vectors[2:3]
    packed = spare[:, :, 3 : 3 + packed.shape[0]].transpose(0, 2, 1)
    packed = packed.reshape(groups, 2, part, groups).astype(F32).sum(axis=1)
    chosen = jnp.arange(groups, dtype=jnp.int32)
    gates = jnp.sum(jnp.where(chosen == me_ep, packed, 0.0), axis=2)
    order = jnp.stack(relative_to_absolute())
    gates = jnp.sum(jnp.where((order[:, None] == chosen)[:, :, None], gates[None], 0.0), axis=1)
    gates = gates.reshape(groups * part, 1)
    blocks, last = gather_ep(after(output_weight.T, last))
    w_out = stack_absolute(blocks).reshape(width, wide)

    def from_tp(array):
        return stack_static(gather_tp(array)).transpose(1, 0, 2, 3).reshape(3, -1, width)

    routed = from_tp(
        jnp.stack([routed_gate_weight[0].T, routed_up_weight[0].T, expert_down[0]])
    )

    units = shared_down.shape[0]
    piece = units // groups
    shared = jnp.stack([shared_gate.T, shared_up.T, shared_down]).reshape(3, groups, piece, -1)
    shared = lax.all_to_all(after(shared, last), "ep", split_axis=1, concat_axis=1, tiled=True)
    shared = from_tp(shared.transpose(0, 2, 1, 3).reshape(3, piece, width))

    inputs32 = tokens.astype(F32)
    scale_one = rms_scale(inputs32)
    act1 = (inputs32 * scale_one * gain_one32).astype(BF)
    qkv = nn(act1, w_qkv).astype(BF)
    query, key, value = qkv[:, :wide], qkv[:, wide : 2 * wide], qkv[:, 2 * wide :]
    positions = jnp.arange(count, dtype=jnp.int32)
    start = piece_start[0]
    inside = (positions >= start) & (positions < start + piece_length[0])
    visible = (positions[None, :] <= positions[:, None]) | inside[:, None] & inside[None, :]
    all_lse, mixes = [], []
    for h in range(local_heads):
        scores = jnp.where(visible, nt(columns(query, h), columns(key, h)) * factor, -1e30)
        highest = jnp.max(scores, axis=-1, keepdims=True)
        lse = highest + jnp.log(jnp.sum(jnp.exp(scores - highest), axis=-1, keepdims=True))
        probs = jnp.exp(scores - lse).astype(BF)
        all_lse.append(lse)
        mixes.append(nn(probs, columns(value, h)).astype(BF))
    attn_mix = jnp.concatenate(mixes, axis=1)
    branch = nt(attn_mix, w_out).reshape(quarters, part, width)
    attn_branch = scatter_tp_rows(branch)

    inputs_own = own(tokens).astype(F32)
    resid = inputs_own + attn_branch
    scale_two = rms_scale(resid)
    act2 = (resid * scale_two * gain_two32).astype(BF)

    blocks, last = gather_ep(act2)
    act_all = stack_static(blocks).reshape(groups * part, width)
    blocks, _ = gather_ep(after(own(block_grad), last))
    gout_all = stack_static(blocks).reshape(groups * part, width)
    ffn_part, gact_part, logit_part, sums = experts(
        act_all, gout_all, gates, logit32, tuple(routed), tuple(shared)
    )
    gact_part = gact_part.reshape(groups, part, width)
    gact2 = scatter_ep(lambda r: gact_part[r])
    ffn_part = after(ffn_part, gact2).reshape(groups, part, width)
    ffn_branch = scatter_ep(lambda r: ffn_part[r])
    block_sum = resid + ffn_branch
    block_out = gather_tp_rows(block_sum.astype(BF))
    squares = jnp.stack(
        [
            jnp.sum(attn_branch * attn_branch),
            jnp.sum(ffn_branch * ffn_branch),
            jnp.sum(block_sum * block_sum),
        ]
    )
    rms_values = jnp.sqrt(sum_tp(squares) / (count * width))[None, :]

    def from_hidden(arrays):
        parts = [array.astype(BF).reshape(quarters, -1, width) for array in arrays]
        return scatter_tp(lambda j: jnp.stack([array[j] for array in parts]))

    shared_grads = from_hidden(sums[3:])
    gate_grad, up_grad, down_grad = from_hidden([after(x, shared_grads) for x in sums[:3]])
    gate_grad, up_grad = gate_grad.T, up_grad.T
    shared_grads = shared_grads.astype(BF).reshape(3, piece, groups, -1).transpose(0, 2, 1, 3)
    shared_grads = lax.all_to_all(shared_grads, "ep", split_axis=1, concat_axis=1, tiled=True)
    shared_grads = shared_grads.reshape(3, units, -1)
    sgate_grad = shared_grads[0].T.astype(F32)
    sup_grad = shared_grads[1].T.astype(F32)
    sdown_grad = shared_grads[2].astype(F32)

    resid_part, gain_two_part = norm_back(gact2, resid, scale_two, gain_two32)
    gresid = own(block_grad).astype(F32) + resid_part
    gattn = gather_tp_rows(gresid.astype(BF))
    vectors = jnp.stack([gain_two_part, logit_part], axis=1).reshape(groups, -1, 2)
    vectors = jnp.pad(vectors, ((0, 0), (0, 0), (0, 126))).astype(BF)
    out_grads = tn(gattn, attn_mix).astype(BF).reshape(groups, -1, wide)
    out_grads = scatter_absolute(jnp.concatenate([out_grads, vectors], axis=2))
    output_grad = out_grads[:, :wide].T
    early = sum_tp(out_grads[:, wide : wide + 2])
    gmix = nn(gattn, w_out).astype(BF)
    gqs, gks, gvs = [], [], []
    for h in range(local_heads):
        query_h, key_h, gmix_h = columns(query, h), columns(key, h), columns(gmix, h)
        scores = jnp.where(visible, nt(query_h, key_h) * factor, -1e30)
        probs = jnp.exp(scores - all_lse[h])
        gprob = nt(gmix_h, columns(value, h))
        gvs.append(tn(probs.astype(BF), gmix_h).astype(BF))
        inner = jnp.sum(probs * gprob, axis=-1, keepdims=True)
        gscores = (probs * (gprob - inner)).astype(BF)
        gqs.append((nn(gscores, key_h) * factor).astype(BF))
        gks.append((tn(gscores, query_h) * factor).astype(BF))
    gqkv = jnp.concatenate(gqs + gks + gvs, axis=1)
    gqkv_grad = tn(act1, gqkv).astype(BF).reshape(groups, -1, 3 * wide)
    qkv_grad = scatter_absolute(after(gqkv_grad, out_grads))
    gact1 = nt(gqkv, w_qkv[:, : 3 * wide]).astype(BF).reshape(quarters, part, width)
    gact1 = scatter_tp_rows(gact1)
    input_part, gain_one_part = norm_back(gact1, inputs_own, own(scale_one), gain_one32)
    tokens_grad = gather_tp_rows((gresid + input_part).astype(BF)).astype(F32)

    late = gain_one_part.reshape(groups, -1)
    late = sum_tp(scatter_absolute(late))
    return (
        block_out,
        tokens_grad,
        late,
        qkv_grad[:, :wide],
        qkv_grad[:, wide : 2 * wide],
        qkv_grad[:, 2 * wide :],
        output_grad,
        early[:, 0],
        early[:, 1],
        sgate_grad,
        sup_grad,
        sdown_grad,
        gate_grad[None],
        up_grad[None],
        down_grad[None],
        rms_values,
    )


def solution(mesh):
    in_specs = (
        P("ep", None),
        P("ep"),
        P("ep", "tp"),
        P("ep", "tp"),
        P("ep", "tp"),
        P("tp", "ep"),
        P("ep"),
        P("ep"),
        P("ep", "tp"),
        P("ep", "tp"),
        P("tp", "ep"),
        P("ep", None, "tp"),
        P("ep", None, "tp"),
        P("ep", "tp", None),
        P("ep", None),
        P("ep", None),
        P("ep"),
        P("ep"),
        P("ep", None),
    )
    out_specs = (
        P("ep", None),
        P("ep", None),
        P("ep"),
        P("ep", "tp"),
        P("ep", "tp"),
        P("ep", "tp"),
        P("tp", "ep"),
        P("ep"),
        P("ep"),
        P("ep", "tp"),
        P("ep", "tp"),
        P("tp", "ep"),
        P("ep", None, "tp"),
        P("ep", None, "tp"),
        P("ep", "tp", None),
        P("ep", None),
    )
    return jax.shard_map(
        on_device, mesh=mesh, in_specs=in_specs, out_specs=out_specs, check_vma=False
    )
```

```python
import jax
import jax.numpy as jnp
from jax import lax
from jax.sharding import PartitionSpec as P

HD = 128
EPS = 1e-06
BF = jnp.bfloat16
F32 = jnp.float32


def nn(left, right):
    return lax.dot_general(left, right, (((1,), (0,)), ((), ())), preferred_element_type=F32)


def nt(left, right):
    return lax.dot_general(left, right, (((1,), (1,)), ((), ())), preferred_element_type=F32)


def tn(left, right):
    return lax.dot_general(left, right, (((0,), (0,)), ((), ())), preferred_element_type=F32)


def at(array, index):
    return lax.dynamic_index_in_dim(array, index, 0, keepdims=False)


def put(array, value, index):
    return lax.dynamic_update_index_in_dim(array, value, index, 0)


def after(value, *earlier):
    return lax.optimization_barrier((value,) + earlier)[0]


def swap_inner(value):
    size = lax.axis_size("ep")
    return lax.ppermute(value, "ep", [(i, i ^ 1) for i in range(size)])


def ring_outer(value):
    size = lax.axis_size("ep")
    return lax.ppermute(value, "ep", [(i, (i + 2) % size) for i in range(size)])


def swap_tp(value, mask):
    size = lax.axis_size("tp")
    return lax.ppermute(value, "tp", [(i, i ^ mask) for i in range(size)])


def relative_to_absolute():
    size = lax.axis_size("ep")
    me = lax.axis_index("ep")
    outer, inner = me // 2, me % 2
    rounds = size // 2
    return [(outer + rounds - r // 2) % rounds * 2 + (inner ^ r % 2) for r in range(size)]


def gather_ep(shard, works=()):
    rounds = lax.axis_size("ep") // 2
    blocks, done = [], []
    current = shard
    for k in range(rounds):
        other = swap_inner(current)
        following = ring_outer(current) if k < rounds - 1 else None
        if k < len(works):
            result = works[k](current)
            done.append(result)
            other = after(other, *jax.tree.leaves(result))
        blocks += [current, other]
        if following is not None:
            current = after(following, other)
    return (blocks, done + [work(other) for work in works[rounds:]]) if works else blocks


def stack_static(blocks):
    whole = jnp.zeros((len(blocks),) + blocks[0].shape, blocks[0].dtype)
    for i, block in enumerate(blocks):
        whole = whole.at[i].set(block)
    return whole


def stack_absolute(blocks):
    whole = jnp.zeros((len(blocks),) + blocks[0].shape, blocks[0].dtype)
    for block, index in zip(blocks, relative_to_absolute()):
        whole = put(whole, block, index)
    return whole


def scatter_ep(block_of, works=()):
    rounds = lax.axis_size("ep") // 2
    arrived = other = token = None
    done = []
    for step, k in enumerate(list(range(1, rounds)) + [0]):
        away = block_of(2 * k + 1).astype(BF)
        if other is not None:
            away = after(away, other)
        other = swap_inner(away)
        if step < len(works):
            result = works[step](token)
            done.append(result)
            other = after(other, *jax.tree.leaves(result))
        total = block_of(2 * k).astype(F32) + other.astype(F32)
        if arrived is not None:
            total = total + arrived.astype(F32)
        if k:
            token = total.astype(BF)
            arrived = ring_outer(token)
    done += [work(total) for work in works[rounds:]]
    return (total, done) if works else total


def scatter_absolute(parts, works=()):
    order = relative_to_absolute()
    return scatter_ep(lambda r: at(parts, order[r]), works)


TP_ORDER = (0, 2, 1, 3)


def gather_tp(shard):
    far = swap_tp(shard, 2)
    return [shard, far, swap_tp(shard, 1), swap_tp(far, 1)]


def gather_tp_rows(shard):
    me = lax.axis_index("tp")
    whole = jnp.zeros((lax.axis_size("tp"),) + shard.shape, shard.dtype)
    for j, block in zip(TP_ORDER, gather_tp(shard)):
        whole = put(whole, block, me ^ j)
    return whole.reshape(-1, shard.shape[-1])


def scatter_tp(parts):
    near = parts[0].astype(F32) + swap_tp(parts[1], 1).astype(F32)
    return near[0] + swap_tp(near[1].astype(BF), 2).astype(F32)


def scatter_tp_rows(parts):
    me = lax.axis_index("tp")
    far = at(parts, me ^ 2).astype(F32) + swap_tp(at(parts, me ^ 3).astype(BF), 1).astype(F32)
    far = swap_tp(far.astype(BF), 2)
    near = swap_tp(at(parts, me ^ 1).astype(BF), 1)
    return at(parts, me).astype(F32) + near.astype(F32) + far.astype(F32)


def sum_tp(value):
    value = value + swap_tp(value, 1)
    return value + swap_tp(value, 2)


def rms_scale(values):
    return lax.rsqrt(jnp.mean(values * values, axis=-1, keepdims=True) + EPS)


def norm_back(grad, values, scale, gain):
    weighted = grad * gain
    inner = jnp.mean(values * weighted, axis=-1, keepdims=True)
    return (scale * weighted - values * scale**3 * inner, jnp.sum(grad * values * scale, axis=0))


def gated_back(grad_hidden, gate_val, up_val):
    squash = jax.nn.sigmoid(gate_val)
    grad_gate = grad_hidden * up_val * squash * (1.0 + gate_val * (1.0 - squash))
    grad_up = grad_hidden * gate_val * squash
    return (grad_gate.astype(BF), grad_up.astype(BF))


def group_forward(act, coef, group):
    gate_val, up_val = nt(act, group[0]), nt(act, group[1])
    return gate_val, up_val, (jax.nn.silu(gate_val) * up_val * coef).astype(BF)


def group_back(gout, coef, kept, group):
    return gated_back(nt(gout, group[2]) * coef, kept[0], kept[1])


def score_of(act, logit32):
    return jax.nn.sigmoid(jnp.sum(act.astype(F32) * logit32, axis=1, keepdims=True))


def score_back(gout, score, kept, group):
    plain = jax.nn.silu(kept[0]) * kept[1]
    return score * (1.0 - score) * jnp.sum(plain * nt(gout, group[2]), axis=1, keepdims=True)


def hidden_to_rows(hidden, groups):
    return sum(nn(h, group[2]) for h, group in zip(hidden, groups)).astype(BF)


def grads_to_rows(grads, gscore, logit32, groups):
    total = sum(nn(g[0], group[0]) + nn(g[1], group[1]) for g, group in zip(grads, groups))
    return (total + gscore * logit32).astype(BF)


def expert_step(act, gout, gates, logit32, groups):
    score = score_of(act, logit32)
    coefs = [gates] * (len(groups) - 1) + [score]
    kept = [group_forward(act, c, group) for c, group in zip(coefs, groups)]
    out = hidden_to_rows([k[2] for k in kept], groups)
    grads = [group_back(gout, c, k, group) for c, k, group in zip(coefs, kept, groups)]
    gscore = score_back(gout, score, kept[-1], groups[-1])
    gact = grads_to_rows(grads, gscore, logit32, groups)
    sums = [jnp.sum(act.astype(F32) * gscore, axis=0)]
    for g, k in zip(grads, kept):
        sums += [tn(g[0], act), tn(g[1], act), tn(k[2], gout)]
    return out, gact, tuple(sums)


def experts_in_blocks(act, gout, gates, logit32, groups, steps):
    rows, width = act.shape

    def step(totals, block):
        out, gact, sums = expert_step(*block, logit32, groups)
        return tuple(t + s for t, s in zip(totals, sums)), (out, gact)

    blocks = tuple(x.reshape(steps, rows // steps, -1) for x in (act, gout, gates))
    sizes = [(width,)] + [w.shape for group in groups for w in group]
    totals = tuple(jnp.zeros(size, F32) for size in sizes)
    sums, (out, gact) = lax.scan(step, totals, blocks)
    return out.reshape(rows, width), gact.reshape(rows, width), sums[0], sums[1:]


def columns(array, head):
    return array[:, head * HD : (head + 1) * HD]


def on_device(
    tokens,
    first_gain,
    query_weight,
    key_weight,
    value_weight,
    output_weight,
    second_gain,
    shared_logit,
    shared_gate,
    shared_up,
    shared_down,
    routed_gate_weight,
    routed_up_weight,
    expert_down,
    route_ids,
    route_gates,
    piece_start,
    piece_length,
    block_grad,
):
    groups = lax.axis_size("ep")
    quarters = lax.axis_size("tp")
    me_ep = lax.axis_index("ep")
    me_tp = lax.axis_index("tp")
    count, width = tokens.shape
    part = count // quarters
    local_heads = query_weight.shape[1] // HD
    wide = local_heads * HD
    factor = HD ** (-0.5)

    def own(array):
        return lax.dynamic_slice_in_dim(array, me_tp * part, part, 0)

    dense = jnp.sum(
        own(route_gates)[:, :, None]
        * (own(route_ids)[:, :, None] == jnp.arange(groups, dtype=jnp.int32)).astype(F32),
        axis=1,
    )
    rows = query_weight.shape[0]
    high = dense.astype(BF)
    low = (dense - high.astype(F32)).astype(BF)
    packed = jnp.concatenate([high.reshape(-1), low.reshape(-1)]).reshape(-1, rows)
    spare = jnp.concatenate([jnp.stack([first_gain, second_gain, shared_logit]), packed]).T
    spare = jnp.pad(spare, ((0, 0), (0, -spare.shape[1] % 128)))
    blocks = gather_ep(
        jnp.concatenate(
            [query_weight, key_weight, value_weight, output_weight.T, spare], axis=1
        )
    )
    weights = stack_absolute(blocks)
    spare = weights[:, :, 4 * wide :]
    weights = weights.reshape(width, -1)
    w_qkv, w_out = weights[:, : 3 * wide], weights[:, 3 * wide : 4 * wide]
    vectors = spare[:, :, :3].reshape(width, 3).T.astype(F32)
    gain_one32, gain_two32, logit32 = vectors[0:1], vectors[1:2], vectors[2:3]
    packed = spare[:, :, 3 : 3 + packed.shape[0]].transpose(0, 2, 1)
    packed = packed.reshape(groups, 2, part, groups).astype(F32).sum(axis=1)
    chosen = jnp.arange(groups, dtype=jnp.int32)
    gates = jnp.sum(jnp.where(chosen == me_ep, packed, 0.0), axis=2)
    order = jnp.stack(relative_to_absolute())
    gates = jnp.sum(jnp.where((order[:, None] == chosen)[:, :, None], gates[None], 0.0), axis=1)
    gates = gates.reshape(groups * part, 1)

    def from_tp(array):
        parts = gather_tp(array)

        def joined(chosen, i):
            return stack_static([part[i] for part in chosen]).reshape(-1, width)

        return parts, joined

    routed_gate, routed_up, routed_down = lax.optimization_barrier(
        (routed_gate_weight[0], routed_up_weight[0], expert_down[0], blocks[0])
    )[:3]
    parts, joined = from_tp(jnp.stack([routed_gate.T, routed_up.T, routed_down]))
    near_group = tuple(joined(parts[:2], i) for i in range(3))
    far_group = tuple(joined(parts[2:], i) for i in range(3))

    units = shared_down.shape[0]
    piece = units // groups
    shared = jnp.stack([shared_gate.T, shared_up.T, shared_down]).reshape(3, groups, piece, -1)
    shared = lax.all_to_all(after(shared, blocks[-1]), "ep", split_axis=1, concat_axis=1, tiled=True)
    parts, joined = from_tp(shared.transpose(0, 2, 1, 3).reshape(3, piece, width))
    shared_group = tuple(joined(parts, i) for i in range(3))
    units_of = (near_group, far_group, shared_group)

    inputs32 = tokens.astype(F32)
    scale_one = rms_scale(inputs32)
    act1 = (inputs32 * scale_one * gain_one32).astype(BF)
    qkv = nn(act1, w_qkv).astype(BF)
    query, key, value = qkv[:, :wide], qkv[:, wide : 2 * wide], qkv[:, 2 * wide :]
    positions = jnp.arange(count, dtype=jnp.int32)
    start = piece_start[0]
    inside = (positions >= start) & (positions < start + piece_length[0])
    visible = (positions[None, :] <= positions[:, None]) | inside[:, None] & inside[None, :]
    all_lse, mixes = [], []
    for h in range(local_heads):
        scores = jnp.where(visible, nt(columns(query, h), columns(key, h)) * factor, -1e30)
        highest = jnp.max(scores, axis=-1, keepdims=True)
        lse = highest + jnp.log(jnp.sum(jnp.exp(scores - highest), axis=-1, keepdims=True))
        probs = jnp.exp(scores - lse).astype(BF)
        all_lse.append(lse)
        mixes.append(nn(probs, columns(value, h)).astype(BF))
    attn_mix = jnp.concatenate(mixes, axis=1)
    branch = nt(attn_mix, w_out).reshape(quarters, part, width)
    attn_branch = scatter_tp_rows(branch)

    inputs_own = own(tokens).astype(F32)
    resid = inputs_own + attn_branch
    scale_two = rms_scale(resid)
    act2 = (resid * scale_two * gain_two32).astype(BF)

    act_all = stack_static(gather_ep(act2)).reshape(groups * part, width)
    gout_own = after(own(block_grad), act_all)

    def tokens_back(block):
        return block.reshape(groups, part, width)

    def prepare_shared(total):
        total = total.astype(BF).reshape(3, piece, groups, -1).transpose(0, 2, 1, 3)
        return lax.optimization_barrier(total)

    steps = -(-groups * part // 768)
    if steps == 1:
        score = score_of(act_all, logit32)
        coefs = (gates, gates, score)
        kept, grads = [], []

        def forward(i):
            def run(token):
                kept.append(group_forward(after(act_all, token), coefs[i], units_of[i]))
                return kept[-1]

            return run

        def output(token):
            return hidden_to_rows([k[2] for k in kept], units_of)

        blocks, done = gather_ep(gout_own, [forward(0), forward(1), forward(2), output])
        gout_all = stack_static(blocks).reshape(groups * part, width)
        ffn_part = tokens_back(done[-1])

        def backward(i):
            def run(token):
                gout = gout_all if token is None else after(gout_all, token)
                grads.append(group_back(gout, coefs[i], kept[i], units_of[i]))
                if i < 2:
                    return grads[-1]
                return grads[-1], score_back(gout, score, kept[i], units_of[i])

            return run

        def rows_back(token):
            return grads_to_rows(grads, done_back[0], logit32, units_of)

        done_back = []

        def last_backward(token):
            result = backward(2)(token)
            done_back.append(result[1])
            return result

        ffn_branch, done = scatter_ep(
            lambda r: ffn_part[r], [backward(0), backward(1), last_backward, rows_back]
        )
        gscore = done_back[0]
        gact_part = after(tokens_back(done[-1]), ffn_branch)
        hidden = [k[2] for k in kept]

        def weight_grads(i, act, gout):
            return [
                tn(grads[i][0], act).astype(BF),
                tn(grads[i][1], act).astype(BF),
                tn(hidden[i], gout).astype(BF),
            ]

        state = {}

        def shared_grads_work(token):
            act, gout = lax.optimization_barrier((act_all, gout_all, gact_part))[:2]
            state["shared"] = weight_grads(2, act, gout)
            away = jnp.stack([w[2 * piece :] for w in state["shared"]])
            state["shared_got"] = swap_tp(away, 1)
            state["logit"] = jnp.sum(act.astype(F32) * gscore, axis=0)
            return away, state["logit"]

        def far_work(token):
            act, gout = lax.optimization_barrier((act_all, gout_all, token))[:2]
            away = weight_grads(1, act, gout)
            state["got"] = [swap_tp(w, 1) for w in away]
            return away

        def near_work(token):
            along_x = jnp.stack([w[piece : 2 * piece] for w in state["shared"]]).astype(F32)
            along_x = (along_x + state["shared_got"][:, piece:].astype(F32)).astype(BF)
            state["shared_x"] = swap_tp(along_x, 2)
            act = lax.optimization_barrier((act_all, token, along_x))[0]
            state["near"] = [tn(grads[0][0], act).astype(BF), tn(grads[0][1], act).astype(BF)]
            return state["near"]

        def quarter_x(i):
            rows = routed_down.shape[0]
            return (
                state["near"][i][rows:].astype(F32) + state["got"][i][rows:].astype(F32)
            ).astype(BF)

        def down_work(token):
            along_x = [quarter_x(0), quarter_x(1)]
            state["x"] = [swap_tp(a, 2) for a in along_x]
            gout = lax.optimization_barrier((gout_all, token, *along_x))[0]
            state["near"].append(tn(hidden[0], gout).astype(BF))
            return state["near"][2]

        gact2, _ = scatter_ep(
            lambda r: gact_part[r], [shared_grads_work, far_work, near_work, down_work]
        )
        along_x = quarter_x(2)
        state["x"].append(swap_tp(along_x, 2))
        logit_part = state["logit"]

        def own_grad(i):
            rows = routed_down.shape[0]
            total = state["near"][i][:rows].astype(F32) + state["got"][i][:rows].astype(F32)
            return total + state["x"][i].astype(F32)

        def shared_total():
            total = jnp.stack([w[:piece] for w in state["shared"]]).astype(F32)
            total = total + state["shared_got"][:, :piece].astype(F32)
            return prepare_shared(total + state["shared_x"].astype(F32))

        def expert_grads():
            return own_grad(0), own_grad(1), own_grad(2)

    else:
        gout_all = stack_static(gather_ep(gout_own)).reshape(groups * part, width)
        ffn_part, gact_part, logit_part, sums = experts_in_blocks(
            act_all, gout_all, gates, logit32, units_of, steps
        )
        ffn_part, gact_part = tokens_back(ffn_part), tokens_back(gact_part)
        gact2 = scatter_ep(lambda r: gact_part[r])
        ffn_branch = scatter_ep(lambda r: ffn_part[r])
        along_x = sums[0]

        def expert_grads():
            pairs = [jnp.stack([a.astype(BF), b.astype(BF)]) for a, b in zip(sums[:3], sums[3:6])]
            return [scatter_tp(pair.reshape(2, 2, -1, width)) for pair in pairs]

        def shared_total():
            parts = [w.reshape(2, 2, -1, width).astype(BF) for w in sums[6:]]
            return prepare_shared(jnp.stack([scatter_tp(w) for w in parts]))

    block_sum = resid + ffn_branch
    block_out = gather_tp_rows(block_sum.astype(BF))
    squares = jnp.stack(
        [
            jnp.sum(attn_branch * attn_branch),
            jnp.sum(ffn_branch * ffn_branch),
            jnp.sum(block_sum * block_sum),
        ]
    )
    rms_values = jnp.sqrt(sum_tp(squares) / (count * width))[None, :]

    resid_part, gain_two_part = norm_back(gact2, resid, scale_two, gain_two32)
    gresid = own(block_grad).astype(F32) + resid_part
    gattn = after(gather_tp_rows(gresid.astype(BF)), along_x)
    vectors = jnp.stack([gain_two_part, logit_part], axis=1).reshape(groups, -1, 2)
    vectors = jnp.pad(vectors, ((0, 0), (0, 0), (0, 126))).astype(BF)
    out_grads = tn(gattn, attn_mix).astype(BF).reshape(groups, -1, wide)
    gmix = nn(gattn, w_out).astype(BF)

    def head_back(h):
        def run(token):
            gmix_h = columns(gmix, h)
            if token is not None:
                gmix_h = after(gmix_h, token)
            if h == local_heads - 2:
                gmix_h = after(gmix_h, shared_grads)
            query_h, key_h = columns(query, h), columns(key, h)
            scores = jnp.where(visible, nt(query_h, key_h) * factor, -1e30)
            probs = jnp.exp(scores - all_lse[h])
            gprob = nt(gmix_h, columns(value, h))
            gvalue = tn(probs.astype(BF), gmix_h).astype(BF)
            inner = jnp.sum(probs * gprob, axis=-1, keepdims=True)
            gscores = (probs * (gprob - inner)).astype(BF)
            gquery = (nn(gscores, key_h) * factor).astype(BF)
            gkey = (tn(gscores, query_h) * factor).astype(BF)
            return gquery, gkey, gvalue

        return run

    shared_grads = shared_total()
    out_grads, heads = scatter_absolute(
        jnp.concatenate([out_grads, vectors], axis=2), [head_back(h) for h in range(local_heads)]
    )
    output_grad = out_grads[:, :wide].T
    early = sum_tp(out_grads[:, wide : wide + 2])
    gqkv = jnp.concatenate([head[i] for i in range(3) for head in heads], axis=1)
    gqkv_grad = tn(act1, gqkv).astype(BF).reshape(groups, -1, 3 * wide)
    qkv_grad = scatter_absolute(gqkv_grad)
    gact1 = nt(after(gqkv, gqkv_grad), w_qkv).astype(BF).reshape(quarters, part, width)
    gact1 = scatter_tp_rows(gact1)
    input_part, _ = norm_back(gact1, inputs_own, own(scale_one), gain_one32)
    tokens_grad = gather_tp_rows((gresid + input_part).astype(BF)).astype(F32)

    shared_grads = lax.all_to_all(shared_grads, "ep", split_axis=1, concat_axis=1, tiled=True)
    shared_grads = shared_grads.reshape(3, units, -1)
    sgate_grad = shared_grads[0].T.astype(F32)
    sup_grad = shared_grads[1].T.astype(F32)
    sdown_grad = shared_grads[2].astype(F32)
    gate_grad, up_grad, down_grad = expert_grads()

    own_qkv = jnp.concatenate([query_weight, key_weight, value_weight], axis=1).astype(F32)
    late = sum_tp(jnp.sum(own_qkv * qkv_grad, axis=1) / first_gain.astype(F32))
    return (
        block_out,
        tokens_grad,
        late,
        qkv_grad[:, :wide],
        qkv_grad[:, wide : 2 * wide],
        qkv_grad[:, 2 * wide :],
        output_grad,
        early[:, 0],
        early[:, 1],
        sgate_grad,
        sup_grad,
        sdown_grad,
        gate_grad.T[None],
        up_grad.T[None],
        down_grad[None],
        rms_values,
    )


def solution(mesh):
    in_specs = (
        P("ep", None),
        P("ep"),
        P("ep", "tp"),
        P("ep", "tp"),
        P("ep", "tp"),
        P("tp", "ep"),
        P("ep"),
        P("ep"),
        P("ep", "tp"),
        P("ep", "tp"),
        P("tp", "ep"),
        P("ep", None, "tp"),
        P("ep", None, "tp"),
        P("ep", "tp", None),
        P("ep", None),
        P("ep", None),
        P("ep"),
        P("ep"),
        P("ep", None),
    )
    out_specs = (
        P("ep", None),
        P("ep", None),
        P("ep"),
        P("ep", "tp"),
        P("ep", "tp"),
        P("ep", "tp"),
        P("tp", "ep"),
        P("ep"),
        P("ep"),
        P("ep", "tp"),
        P("ep", "tp"),
        P("tp", "ep"),
        P("ep", None, "tp"),
        P("ep", None, "tp"),
        P("ep", "tp", None),
        P("ep", None),
    )
    return jax.shard_map(
        on_device, mesh=mesh, in_specs=in_specs, out_specs=out_specs, check_vma=False
    )
```

```python
import jax
import jax.numpy as jnp
from jax import lax
from jax.sharding import PartitionSpec as P

HD = 128
EPS = 1e-06
BF = jnp.bfloat16
F32 = jnp.float32


def nn(left, right):
    return lax.dot_general(left, right, (((1,), (0,)), ((), ())), preferred_element_type=F32)


def nt(left, right):
    return lax.dot_general(left, right, (((1,), (1,)), ((), ())), preferred_element_type=F32)


def tn(left, right):
    return lax.dot_general(left, right, (((0,), (0,)), ((), ())), preferred_element_type=F32)


def at(array, index):
    return lax.dynamic_index_in_dim(array, index, 0, keepdims=False)


def put(array, value, index):
    return lax.dynamic_update_index_in_dim(array, value, index, 0)


def after(value, *earlier):
    return lax.optimization_barrier((value,) + earlier)[0]


def together(value, result):
    leaves, tree = jax.tree.flatten(result)
    value, *leaves = lax.optimization_barrier((value, *leaves))
    return value, jax.tree.unflatten(tree, leaves)


def swap_inner(value):
    size = lax.axis_size("ep")
    return lax.ppermute(value, "ep", [(i, i ^ 1) for i in range(size)])


def ring_outer(value):
    size = lax.axis_size("ep")
    return lax.ppermute(value, "ep", [(i, (i + 2) % size) for i in range(size)])


def swap_tp(value, mask):
    size = lax.axis_size("tp")
    return lax.ppermute(value, "tp", [(i, i ^ mask) for i in range(size)])


def relative_to_absolute():
    size = lax.axis_size("ep")
    me = lax.axis_index("ep")
    outer, inner = me // 2, me % 2
    rounds = size // 2
    return [(outer + rounds - r // 2) % rounds * 2 + (inner ^ r % 2) for r in range(size)]


def gather_ep(shard, works=()):
    rounds = lax.axis_size("ep") // 2
    blocks, done = [], []
    current = shard
    for k in range(rounds):
        other = swap_inner(current)
        following = ring_outer(current) if k < rounds - 1 else None
        if k < len(works):
            other, result = together(other, works[k](current))
            done.append(result)
        blocks += [current, other]
        if following is not None:
            current = after(following, other)
    return (blocks, done + [work(other) for work in works[rounds:]]) if works else blocks


def stack_static(blocks):
    whole = jnp.zeros((len(blocks),) + blocks[0].shape, blocks[0].dtype)
    for i, block in enumerate(blocks):
        whole = whole.at[i].set(block)
    return whole


def stack_absolute(blocks):
    whole = jnp.zeros((len(blocks),) + blocks[0].shape, blocks[0].dtype)
    for block, index in zip(blocks, relative_to_absolute()):
        whole = put(whole, block, index)
    return whole


def scatter_ep(block_of, works=()):
    rounds = lax.axis_size("ep") // 2
    arrived = other = token = None
    done = []
    for step, k in enumerate(list(range(1, rounds)) + [0]):
        away = block_of(2 * k + 1).astype(BF)
        if other is not None:
            away = after(away, other)
        other = swap_inner(away)
        if step < len(works):
            other, result = together(other, works[step](token))
            done.append(result)
        total = block_of(2 * k).astype(F32) + other.astype(F32)
        if arrived is not None:
            total = total + arrived.astype(F32)
        if k:
            token = total.astype(BF)
            arrived = ring_outer(token)
    done += [work(total) for work in works[rounds:]]
    return (total, done) if works else total


def scatter_absolute(parts, works=()):
    order = relative_to_absolute()
    return scatter_ep(lambda r: at(parts, order[r]), works)


TP_ORDER = (0, 2, 1, 3)


def gather_tp(shard):
    far = swap_tp(shard, 2)
    return [shard, far, swap_tp(shard, 1), swap_tp(far, 1)]


def gather_tp_rows(shard):
    me = lax.axis_index("tp")
    whole = jnp.zeros((lax.axis_size("tp"),) + shard.shape, shard.dtype)
    for j, block in zip(TP_ORDER, gather_tp(shard)):
        whole = put(whole, block, me ^ j)
    return whole.reshape(-1, shard.shape[-1])


def scatter_tp(parts):
    near = parts[0].astype(F32) + swap_tp(parts[1], 1).astype(F32)
    return near[0] + swap_tp(near[1].astype(BF), 2).astype(F32)


def scatter_tp_rows(parts):
    me = lax.axis_index("tp")
    far = at(parts, me ^ 2).astype(F32) + swap_tp(at(parts, me ^ 3).astype(BF), 1).astype(F32)
    far = swap_tp(far.astype(BF), 2)
    near = swap_tp(at(parts, me ^ 1).astype(BF), 1)
    return at(parts, me).astype(F32) + near.astype(F32) + far.astype(F32)


def scatter_tp_rows_start(parts):
    me = lax.axis_index("tp")
    far = at(parts, me ^ 2).astype(F32) + swap_tp(at(parts, me ^ 3).astype(BF), 1).astype(F32)
    return at(parts, me), swap_tp(at(parts, me ^ 1).astype(BF), 1), swap_tp(far.astype(BF), 2)


def sum_tp(value):
    value = value + swap_tp(value, 1)
    return value + swap_tp(value, 2)


def rms_scale(values):
    return lax.rsqrt(jnp.mean(values * values, axis=-1, keepdims=True) + EPS)


def norm_back(grad, values, scale, gain):
    weighted = grad * gain
    inner = jnp.mean(values * weighted, axis=-1, keepdims=True)
    return (scale * weighted - values * scale**3 * inner, jnp.sum(grad * values * scale, axis=0))


def gated_back(grad_hidden, gate_val, up_val):
    squash = jax.nn.sigmoid(gate_val)
    grad_gate = grad_hidden * up_val * squash * (1.0 + gate_val * (1.0 - squash))
    grad_up = grad_hidden * gate_val * squash
    return (grad_gate.astype(BF), grad_up.astype(BF))


def unit_coefs(gates, score, units, routed):
    return jnp.where(jnp.arange(units.shape[1]) < routed, gates, score)


def expert_forward(act, coef, units):
    gate_val, up_val = nt(act, units[0]), nt(act, units[1])
    return gate_val, up_val, (jax.nn.silu(gate_val) * up_val * coef).astype(BF)


def expert_back(gout, coef, score, kept, units, routed):
    grad_plain = nt(gout, units[2])
    plain = (jax.nn.silu(kept[0]) * kept[1])[:, routed:] * grad_plain[:, routed:]
    gscore = score * (1.0 - score) * jnp.sum(plain, axis=1, keepdims=True)
    return gated_back(grad_plain * coef, kept[0], kept[1]), gscore


def score_of(act, logit32):
    return jax.nn.sigmoid(jnp.sum(act.astype(F32) * logit32, axis=1, keepdims=True))


def grads_to_rows(grads, gscore, logit32, units):
    total = nn(grads[0], units[0]) + nn(grads[1], units[1])
    return (total + gscore * logit32).astype(BF)


def expert_step(act, gout, gates, logit32, units, routed):
    score = score_of(act, logit32)
    coef = unit_coefs(gates, score, units, routed)
    kept = expert_forward(act, coef, units)
    out = nn(kept[2], units[2]).astype(BF)
    grads, gscore = expert_back(gout, coef, score, kept, units, routed)
    gact = grads_to_rows(grads, gscore, logit32, units)
    logit_part = jnp.sum(act.astype(F32) * gscore, axis=0)
    return out, gact, (logit_part, tn(grads[0], act), tn(grads[1], act), tn(kept[2], gout))


def experts_in_blocks(act, gout, gates, logit32, units, routed, steps):
    rows, width = act.shape

    def step(totals, block):
        out, gact, sums = expert_step(*block, logit32, units, routed)
        return tuple(t + s for t, s in zip(totals, sums)), (out, gact)

    blocks = tuple(x.reshape(steps, rows // steps, -1) for x in (act, gout, gates))
    totals = tuple(jnp.zeros(size, F32) for size in [(width,)] + 3 * [units.shape[1:]])
    sums, (out, gact) = lax.scan(step, totals, blocks)
    return out.reshape(rows, width), gact.reshape(rows, width), sums[0], sums[1:]


def place(units, parts, offset):
    for i, part in parts:
        start = (0, offset + i * part.shape[1], 0)
        units = lax.dynamic_update_slice(units, part, start)
    return units


def columns(array, head):
    return array[:, head * HD : (head + 1) * HD]


def on_device(
    tokens,
    first_gain,
    query_weight,
    key_weight,
    value_weight,
    output_weight,
    second_gain,
    shared_logit,
    shared_gate,
    shared_up,
    shared_down,
    routed_gate_weight,
    routed_up_weight,
    expert_down,
    route_ids,
    route_gates,
    piece_start,
    piece_length,
    block_grad,
):
    groups = lax.axis_size("ep")
    quarters = lax.axis_size("tp")
    me_ep = lax.axis_index("ep")
    me_tp = lax.axis_index("tp")
    count, width = tokens.shape
    part = count // quarters
    local_heads = query_weight.shape[1] // HD
    wide = local_heads * HD
    factor = HD ** (-0.5)

    def own(array):
        return lax.dynamic_slice_in_dim(array, me_tp * part, part, 0)

    dense = jnp.sum(
        own(route_gates)[:, :, None]
        * (own(route_ids)[:, :, None] == jnp.arange(groups, dtype=jnp.int32)).astype(F32),
        axis=1,
    )
    shard_rows = query_weight.shape[0]
    high = dense.astype(BF)
    low = (dense - high.astype(F32)).astype(BF)
    packed = jnp.concatenate([high.reshape(-1), low.reshape(-1)]).reshape(-1, shard_rows)
    first = jnp.pad(first_gain[:, None], ((0, 0), (0, 127)))
    projection = jnp.concatenate([query_weight, key_weight, value_weight, first], axis=1)

    routed_gate, routed_up, routed_down = lax.optimization_barrier(
        (routed_gate_weight[0], routed_up_weight[0], expert_down[0], projection)
    )[:3]
    own_units = jnp.stack([routed_gate.T, routed_up.T, routed_down])
    rows = own_units.shape[1]
    routed = quarters * rows
    units_dev = shared_down.shape[0]
    piece = units_dev // groups
    x_units = swap_tp(own_units, 2)
    core_units = swap_tp(own_units, 1)

    def near_units(block):
        own_part, units = lax.optimization_barrier(
            (own_units, jnp.zeros((3, routed + quarters * piece, width), BF), block)
        )[:2]
        return place(units, [(0, own_part), (2, core_units)], 0)

    def nothing(block):
        return ()

    qkv_blocks, done = gather_ep(projection, [nothing, nothing, near_units])
    units = done[2]
    first = stack_absolute([block[:, 3 * wide :] for block in qkv_blocks])
    gain_one32 = first[:, :, 0].reshape(1, width).astype(F32)
    w_qkv = stack_absolute([block[:, : 3 * wide] for block in qkv_blocks]).reshape(width, -1)

    inputs32 = tokens.astype(F32)
    scale_one = rms_scale(inputs32)
    act1 = (inputs32 * scale_one * gain_one32).astype(BF)
    positions = jnp.arange(count, dtype=jnp.int32)
    start = piece_start[0]
    inside = (positions >= start) & (positions < start + piece_length[0])
    visible = (positions[None, :] <= positions[:, None]) | inside[:, None] & inside[None, :]
    all_lse, mixes, projected = [], [], []

    def project(block):
        projected.append(nn(after(act1, block), w_qkv).astype(BF))
        return projected[0]

    def attend(heads):
        def run(block):
            done = []
            for h in heads:
                query_h = after(columns(projected[0], h), block)
                key_h = columns(projected[0], local_heads + h)
                value_h = columns(projected[0], 2 * local_heads + h)
                scores = jnp.where(visible, nt(query_h, key_h) * factor, -1e30)
                highest = jnp.max(scores, axis=-1, keepdims=True)
                total = jnp.sum(jnp.exp(scores - highest), axis=-1, keepdims=True)
                all_lse.append(highest + jnp.log(total))
                probs = jnp.exp(scores - all_lse[h]).astype(BF)
                mixes.append(nn(probs, value_h).astype(BF))
                done += [all_lse[h], mixes[h]]
            return done

        return run

    spare = jnp.concatenate([jnp.stack([second_gain, shared_logit]), packed]).T
    spare = jnp.pad(spare, ((0, 0), (0, -spare.shape[1] % 128)))
    half = local_heads // 2

    shared = jnp.stack([shared_gate.T, shared_up.T, shared_down]).reshape(3, groups, piece, -1)
    shared = lax.all_to_all(
        after(shared, qkv_blocks[-1]), "ep", split_axis=1, concat_axis=1, tiled=True
    )

    def attend_last(block):
        done = attend(range(half, local_heads))(block)
        return done, after(shared.transpose(0, 2, 1, 3).reshape(3, piece, width), block)

    blocks, done = gather_ep(
        after(jnp.concatenate([output_weight.T, spare], axis=1), qkv_blocks[-1]),
        [project, attend(range(half)), attend_last],
    )
    shared = done[2][1]
    x_shared = swap_tp(shared, 2)
    qkv = projected[0]
    query, key, value = qkv[:, :wide], qkv[:, wide : 2 * wide], qkv[:, 2 * wide :]
    spare = stack_absolute([block[:, wide:] for block in blocks])
    w_out = stack_absolute([block[:, :wide] for block in blocks]).reshape(width, -1)
    vectors = spare[:, :, :2].reshape(width, 2).T.astype(F32)
    gain_two32, logit32 = vectors[0:1], vectors[1:2]
    packed = spare[:, :, 2 : 2 + packed.shape[0]].transpose(0, 2, 1)
    packed = packed.reshape(groups, 2, part, groups).astype(F32).sum(axis=1)
    chosen = jnp.arange(groups, dtype=jnp.int32)
    gates = jnp.sum(jnp.where(chosen == me_ep, packed, 0.0), axis=2)
    order = jnp.stack(relative_to_absolute())
    gates = jnp.sum(jnp.where((order[:, None] == chosen)[:, :, None], gates[None], 0.0), axis=1)
    gates = gates.reshape(groups * part, 1)

    attn_mix = jnp.concatenate(mixes, axis=1)
    branch = nt(attn_mix, w_out).reshape(quarters, part, width)
    attn_branch = scatter_tp_rows(branch)
    inputs_own = own(tokens).astype(F32)
    resid = inputs_own + attn_branch
    scale_two = rms_scale(resid)
    act2 = (resid * scale_two * gain_two32).astype(BF)

    def far_units(block):
        x_part = after(x_units, block)
        return place(units, [(1, x_part), (3, swap_tp(x_part, 1))], 0)

    def shared_units(block):
        x_part = after(x_shared, block)
        return [(0, shared), (1, x_part), (2, swap_tp(shared, 1)), (3, swap_tp(x_part, 1))]

    act_blocks, done = gather_ep(act2, [far_units])
    units = place(done[0], shared_units(act_blocks[4 if len(act_blocks) > 4 else -1]), routed)
    act_all = stack_static(act_blocks).reshape(groups * part, width)
    gout_own = after(own(block_grad), act_blocks[-2])

    def tokens_back(block):
        return block.reshape(groups, part, width)

    def prepare_shared(total):
        total = total.astype(BF).reshape(3, piece, groups, -1).transpose(0, 2, 1, 3)
        return lax.optimization_barrier(total)

    steps = -(-groups * part // 768)
    if steps == 1:
        score = score_of(act_all, logit32)
        coef = unit_coefs(gates, score, units, routed)

        def forward_gate(token):
            return nt(after(act_all, token), units[0])

        kept = []

        def forward_up(token):
            up_val = nt(after(act_all, token), units[1])
            hidden = (jax.nn.silu(kept[0]) * up_val * coef).astype(BF)
            return up_val, hidden

        def output(token):
            return nn(after(kept[2], token), units[2]).astype(BF)

        def keep_up(token):
            kept.extend(forward_up(token))
            return kept[1:]

        def keep_gate(token):
            kept.append(forward_gate(token))
            return kept[0]

        blocks, done = gather_ep(
            gout_own, [keep_gate, keep_up, output]
        )
        gate_val = done[0]
        up_val, hidden = done[1]
        ffn_part = done[2]
        gout_all = stack_static(blocks).reshape(groups * part, width)
        ffn_part = tokens_back(ffn_part)
        back = {}

        def backward(token):
            back["grads"], back["gscore"] = expert_back(
                gout_all, coef, score, (gate_val, up_val), units, routed
            )
            return back["grads"], back["gscore"]

        def rows_gate(token):
            back["rows"] = nn(after(back["grads"][0], token), units[0])
            return back["rows"]

        def rows_up(token):
            total = back["rows"] + nn(after(back["grads"][1], token), units[1])
            return (total + back["gscore"] * logit32).astype(BF)

        state = {"sum": [], "got": [], "x": None}

        def weight_grad(j, token, first, last):
            left = (hidden if j == 2 else back["grads"][j])[:, first:last]
            return tn(left, after(gout_all if j == 2 else act_all, token)).astype(BF)

        def shared_work(token):
            full = jnp.stack([weight_grad(j, token, routed, None) for j in range(3)])
            state["shared"] = full
            away = full[:, 2 * piece :]
            state["shared_got"] = swap_tp(away, 1)
            return away

        def routed_grad(j, token):
            full = weight_grad(j, token, 0, routed)
            away = full[2 * rows :]
            state["sum"].append(full)
            state["got"].append(swap_tp(away, 1))
            return full, away

        def shared_sum(index):
            span = slice(index * piece, (index + 1) * piece)
            return state["shared"][:, span].astype(F32) + state["shared_got"][:, span].astype(F32)

        def summed(j, index):
            span = slice(index * rows, (index + 1) * rows)
            return state["sum"][j][span].astype(F32) + state["got"][j][span].astype(F32)

        def routed_ready(js, token):
            along_x = jnp.concatenate([summed(j, 1) for j in js]).astype(BF)
            state["ready"] = after(along_x, token)
            return state["ready"]

        def routed_x(js, token):
            if "ready" not in state:
                routed_ready(js, token)
            along_x = after(state.pop("ready"), token)
            arrived = swap_tp(along_x, 2)
            state["x"] = arrived if state["x"] is None else jnp.concatenate([state["x"], arrived])
            return along_x

        def gate_work(token):
            along_x = after(shared_sum(1).astype(BF), token)
            state["shared_x"] = swap_tp(along_x, 2)
            return routed_grad(0, token), along_x

        def up_work(token):
            state["logit"] = jnp.sum(after(act_all, token).astype(F32) * back["gscore"], axis=0)
            return routed_grad(1, token), state["logit"]

        def last_work(token):
            return routed_grad(2, token)

        def total_work(token):
            state["total"] = prepare_shared(shared_sum(0) + state["shared_x"].astype(F32))
            return state["total"]

        ffn_branch, done = scatter_ep(
            lambda r: ffn_part[r], [backward, rows_gate, rows_up, shared_work]
        )
        gact_part = tokens_back(done[2])
        gact2, _ = scatter_ep(lambda r: gact_part[r], [gate_work, up_work, nothing, total_work])
        logit_part = state["logit"]

        def shared_total():
            return state["total"]

        def expert_grads():
            arrived = state["x"].reshape(3, rows, width).astype(F32)
            return [summed(j, 0) + arrived[j] for j in range(3)]

    else:
        gout_all = stack_static(gather_ep(gout_own)).reshape(groups * part, width)
        ffn_part, gact_part, logit_part, sums = experts_in_blocks(
            act_all, gout_all, gates, logit32, units, routed, steps
        )
        ffn_part, gact_part = tokens_back(ffn_part), tokens_back(gact_part)
        gact2 = scatter_ep(lambda r: gact_part[r])
        ffn_branch = scatter_ep(lambda r: ffn_part[r])

        def relative(j, first, last):
            parts = sums[j][first:last].reshape(2, 2, -1, width)
            return scatter_tp(parts.astype(BF))

        def last_work(token):
            return ()

        def routed_ready(js, token):
            return ()

        def routed_x(js, token):
            return ()

        def expert_grads():
            return [relative(j, 0, routed) for j in range(3)]

        def shared_total():
            return prepare_shared(jnp.stack([relative(j, routed, None) for j in range(3)]))

    block_sum = resid + ffn_branch
    squares = jnp.stack(
        [
            jnp.sum(attn_branch * attn_branch),
            jnp.sum(ffn_branch * ffn_branch),
            jnp.sum(block_sum * block_sum),
        ]
    )

    resid_part, gain_two_part = norm_back(gact2, resid, scale_two, gain_two32)
    gresid = own(block_grad).astype(F32) + resid_part
    tail = {"shared": shared_total()}
    gresid = after(gresid, tail["shared"])
    gattn = after(gather_tp_rows(gresid.astype(BF)), *jax.tree.leaves(last_work(gresid)))
    block_out = gather_tp_rows(after(block_sum.astype(BF), gattn))
    vectors = jnp.stack([gain_two_part, logit_part], axis=1).reshape(groups, -1, 2)
    vectors = jnp.pad(vectors, ((0, 0), (0, 0), (0, 126))).astype(BF)
    out_grads = tn(gattn, attn_mix).astype(BF).reshape(groups, -1, wide)
    gmix = nn(gattn, w_out).astype(BF)

    def head_back(h):
        def run(token):
            gmix_h = columns(gmix, h)
            if token is not None:
                gmix_h = after(gmix_h, token)
            query_h, key_h = columns(query, h), columns(key, h)
            scores = jnp.where(visible, nt(query_h, key_h) * factor, -1e30)
            probs = jnp.exp(scores - all_lse[h])
            gprob = nt(gmix_h, columns(value, h))
            gvalue = tn(probs.astype(BF), gmix_h).astype(BF)
            inner = jnp.sum(probs * gprob, axis=-1, keepdims=True)
            gscores = (probs * (gprob - inner)).astype(BF)
            gquery = (nn(gscores, key_h) * factor).astype(BF)
            gkey = (tn(gscores, query_h) * factor).astype(BF)
            return gquery, gkey, gvalue

        return run

    def heads_back(first, last):
        def run(token):
            sent = routed_x([0], gattn) if first == 0 else (routed_x([1], token), routed_ready([2], token))
            if first == 0:
                tail["squares"] = sum_tp(after(squares, gattn))
            return [head_back(h)(token) for h in range(first, last)], sent

        return run

    out_grads, heads = scatter_absolute(
        jnp.concatenate([out_grads, vectors], axis=2), [heads_back(0, half), heads_back(half, local_heads)]
    )
    heads = heads[0][0] + heads[1][0]
    output_grad = out_grads[:, :wide].T
    early = sum_tp(out_grads[:, wide : wide + 2])
    gqkv = jnp.concatenate([head[i] for i in range(3) for head in heads], axis=1)
    gqkv_grad = tn(act1, gqkv).astype(BF).reshape(groups, -1, 3 * wide)

    def gact1_work(token):
        shared = lax.all_to_all(tail["shared"], "ep", split_axis=1, concat_axis=1, tiled=True)
        gact1 = nt(after(gqkv, gqkv_grad), w_qkv).astype(BF).reshape(quarters, part, width)
        tail["gact1"] = scatter_tp_rows_start(gact1)
        return gact1, shared

    def tokens_work(token):
        gact1 = sum(part.astype(F32) for part in after(tail["gact1"], token))
        input_part, _ = norm_back(gact1, inputs_own, own(scale_one), gain_one32)
        tail["tokens"] = (gresid + input_part).astype(BF)
        return tail["tokens"], routed_x([2], gact1)

    qkv_grad, done = scatter_absolute(
        gqkv_grad, [gact1_work, tokens_work]
    )
    shared_grads, squares = done[0][1], tail["squares"]
    rms_values = jnp.sqrt(squares / (count * width))[None, :]
    tokens_grad = gather_tp_rows(tail["tokens"]).astype(F32)

    shared_grads = shared_grads.reshape(3, units_dev, -1)
    sgate_grad = shared_grads[0].T.astype(F32)
    sup_grad = shared_grads[1].T.astype(F32)
    sdown_grad = shared_grads[2].astype(F32)
    gate_grad, up_grad, down_grad = expert_grads()

    own_qkv = jnp.concatenate([query_weight, key_weight, value_weight], axis=1).astype(F32)
    late = sum_tp(jnp.sum(own_qkv * qkv_grad, axis=1) / first_gain.astype(F32))
    return (
        block_out,
        tokens_grad,
        late,
        qkv_grad[:, :wide],
        qkv_grad[:, wide : 2 * wide],
        qkv_grad[:, 2 * wide :],
        output_grad,
        early[:, 0],
        early[:, 1],
        sgate_grad,
        sup_grad,
        sdown_grad,
        gate_grad.T[None],
        up_grad.T[None],
        down_grad[None],
        rms_values,
    )


def solution(mesh):
    in_specs = (
        P("ep", None),
        P("ep"),
        P("ep", "tp"),
        P("ep", "tp"),
        P("ep", "tp"),
        P("tp", "ep"),
        P("ep"),
        P("ep"),
        P("ep", "tp"),
        P("ep", "tp"),
        P("tp", "ep"),
        P("ep", None, "tp"),
        P("ep", None, "tp"),
        P("ep", "tp", None),
        P("ep", None),
        P("ep", None),
        P("ep"),
        P("ep"),
        P("ep", None),
    )
    out_specs = (
        P("ep", None),
        P("ep", None),
        P("ep"),
        P("ep", "tp"),
        P("ep", "tp"),
        P("ep", "tp"),
        P("tp", "ep"),
        P("ep"),
        P("ep"),
        P("ep", "tp"),
        P("ep", "tp"),
        P("tp", "ep"),
        P("ep", None, "tp"),
        P("ep", None, "tp"),
        P("ep", "tp", None),
        P("ep", None),
    )
    return jax.shard_map(
        on_device, mesh=mesh, in_specs=in_specs, out_specs=out_specs, check_vma=False
    )
```

```python
import jax
import jax.numpy as jnp
from jax import lax
from jax.sharding import PartitionSpec as P

HD = 128
EPS = 1e-06
BF = jnp.bfloat16
F32 = jnp.float32


def nn(left, right):
    return lax.dot_general(left, right, (((1,), (0,)), ((), ())), preferred_element_type=F32)


def nt(left, right):
    return lax.dot_general(left, right, (((1,), (1,)), ((), ())), preferred_element_type=F32)


def tn(left, right):
    return lax.dot_general(left, right, (((0,), (0,)), ((), ())), preferred_element_type=F32)


def at(array, index):
    return lax.dynamic_index_in_dim(array, index, 0, keepdims=False)


def put(array, value, index):
    return lax.dynamic_update_index_in_dim(array, value, index, 0)


def after(value, *earlier):
    return lax.optimization_barrier((value,) + earlier)[0]


def together(value, result):
    leaves, tree = jax.tree.flatten(result)
    value, *leaves = lax.optimization_barrier((value, *leaves))
    return value, jax.tree.unflatten(tree, leaves)


def swap_inner(value):
    size = lax.axis_size("ep")
    return lax.ppermute(value, "ep", [(i, i ^ 1) for i in range(size)])


def ring_outer(value):
    size = lax.axis_size("ep")
    return lax.ppermute(value, "ep", [(i, (i + 2) % size) for i in range(size)])


def swap_tp(value, mask):
    size = lax.axis_size("tp")
    return lax.ppermute(value, "tp", [(i, i ^ mask) for i in range(size)])


def relative_to_absolute():
    size = lax.axis_size("ep")
    me = lax.axis_index("ep")
    outer, inner = me // 2, me % 2
    rounds = size // 2
    return [(outer + rounds - r // 2) % rounds * 2 + (inner ^ r % 2) for r in range(size)]


def gather_ep(shard, works=()):
    rounds = lax.axis_size("ep") // 2
    blocks, done = [], []
    current = shard
    for k in range(rounds):
        other = swap_inner(current)
        following = ring_outer(current) if k < rounds - 1 else None
        if k < len(works):
            other, result = together(other, works[k](current))
            done.append(result)
        blocks += [current, other]
        if following is not None:
            current = after(following, other)
    return (blocks, done + [work(other) for work in works[rounds:]]) if works else blocks


def stack_static(blocks):
    whole = jnp.zeros((len(blocks),) + blocks[0].shape, blocks[0].dtype)
    for i, block in enumerate(blocks):
        whole = whole.at[i].set(block)
    return whole


def stack_absolute(blocks):
    whole = jnp.zeros((len(blocks),) + blocks[0].shape, blocks[0].dtype)
    for block, index in zip(blocks, relative_to_absolute()):
        whole = put(whole, block, index)
    return whole


def scatter_ep(block_of, works=()):
    rounds = lax.axis_size("ep") // 2
    arrived = other = token = None
    done = []
    for step, k in enumerate(list(range(1, rounds)) + [0]):
        away = block_of(2 * k + 1).astype(BF)
        if other is not None:
            away = after(away, other)
        other = swap_inner(away)
        if step < len(works):
            other, result = together(other, works[step](token))
            done.append(result)
        total = block_of(2 * k).astype(F32) + other.astype(F32)
        if arrived is not None:
            total = total + arrived.astype(F32)
        if k:
            token = total.astype(BF)
            arrived = ring_outer(token)
    done += [work(total) for work in works[rounds:]]
    return (total, done) if works else total


def scatter_absolute(parts, works=()):
    order = relative_to_absolute()
    return scatter_ep(lambda r: at(parts, order[r]), works)


TP_ORDER = (0, 2, 1, 3)


def gather_tp(shard):
    far = swap_tp(shard, 2)
    return [shard, far, swap_tp(shard, 1), swap_tp(far, 1)]


def gather_tp_rows(shard):
    me = lax.axis_index("tp")
    whole = jnp.zeros((lax.axis_size("tp"),) + shard.shape, shard.dtype)
    for j, block in zip(TP_ORDER, gather_tp(shard)):
        whole = put(whole, block, me ^ j)
    return whole.reshape(-1, shard.shape[-1])


def scatter_tp(parts):
    near = parts[0].astype(F32) + swap_tp(parts[1], 1).astype(F32)
    return near[0] + swap_tp(near[1].astype(BF), 2).astype(F32)


def scatter_tp_rows(parts):
    me = lax.axis_index("tp")
    far = at(parts, me ^ 2).astype(F32) + swap_tp(at(parts, me ^ 3).astype(BF), 1).astype(F32)
    far = swap_tp(far.astype(BF), 2)
    near = swap_tp(at(parts, me ^ 1).astype(BF), 1)
    return at(parts, me).astype(F32) + near.astype(F32) + far.astype(F32)


def scatter_tp_rows_start(parts):
    me = lax.axis_index("tp")
    far = at(parts, me ^ 2).astype(F32) + swap_tp(at(parts, me ^ 3).astype(BF), 1).astype(F32)
    return at(parts, me), swap_tp(at(parts, me ^ 1).astype(BF), 1), swap_tp(far.astype(BF), 2)


def sum_tp(value):
    value = value + swap_tp(value, 1)
    return value + swap_tp(value, 2)


def rms_scale(values):
    return lax.rsqrt(jnp.mean(values * values, axis=-1, keepdims=True) + EPS)


def norm_back(grad, values, scale, gain):
    weighted = grad * gain
    inner = jnp.mean(values * weighted, axis=-1, keepdims=True)
    return (scale * weighted - values * scale**3 * inner, jnp.sum(grad * values * scale, axis=0))


def gated_back(grad_hidden, gate_val, up_val):
    squash = jax.nn.sigmoid(gate_val)
    grad_gate = grad_hidden * up_val * squash * (1.0 + gate_val * (1.0 - squash))
    grad_up = grad_hidden * gate_val * squash
    return (grad_gate.astype(BF), grad_up.astype(BF))


def unit_coefs(gates, score, units, routed):
    return jnp.where(jnp.arange(units.shape[1]) < routed, gates, score)


def expert_forward(act, coef, units):
    gate_val, up_val = nt(act, units[0]), nt(act, units[1])
    return gate_val, up_val, (jax.nn.silu(gate_val) * up_val * coef).astype(BF)


def expert_back(gout, coef, score, kept, units, routed):
    grad_plain = nt(gout, units[2])
    plain = (jax.nn.silu(kept[0]) * kept[1])[:, routed:] * grad_plain[:, routed:]
    gscore = score * (1.0 - score) * jnp.sum(plain, axis=1, keepdims=True)
    return gated_back(grad_plain * coef, kept[0], kept[1]), gscore


def score_of(act, logit32):
    return jax.nn.sigmoid(jnp.sum(act.astype(F32) * logit32, axis=1, keepdims=True))


def grads_to_rows(grads, gscore, logit32, units):
    total = nn(grads[0], units[0]) + nn(grads[1], units[1])
    return (total + gscore * logit32).astype(BF)


def expert_step(act, gout, gates, logit32, units, routed):
    score = score_of(act, logit32)
    coef = unit_coefs(gates, score, units, routed)
    kept = expert_forward(act, coef, units)
    out = nn(kept[2], units[2]).astype(BF)
    grads, gscore = expert_back(gout, coef, score, kept, units, routed)
    gact = grads_to_rows(grads, gscore, logit32, units)
    logit_part = jnp.sum(act.astype(F32) * gscore, axis=0)
    return out, gact, (logit_part, tn(grads[0], act), tn(grads[1], act), tn(kept[2], gout))


def experts_in_blocks(act, gout, gates, logit32, units, routed, steps):
    rows, width = act.shape

    def step(totals, block):
        out, gact, sums = expert_step(*block, logit32, units, routed)
        return tuple(t + s for t, s in zip(totals, sums)), (out, gact)

    blocks = tuple(x.reshape(steps, rows // steps, -1) for x in (act, gout, gates))
    totals = tuple(jnp.zeros(size, F32) for size in [(width,)] + 3 * [units.shape[1:]])
    sums, (out, gact) = lax.scan(step, totals, blocks)
    return out.reshape(rows, width), gact.reshape(rows, width), sums[0], sums[1:]


def place(units, parts, offset):
    for i, part in parts:
        start = (0, offset + i * part.shape[1], 0)
        units = lax.dynamic_update_slice(units, part, start)
    return units


def columns(array, head):
    return array[:, head * HD : (head + 1) * HD]


def on_device(
    tokens,
    first_gain,
    query_weight,
    key_weight,
    value_weight,
    output_weight,
    second_gain,
    shared_logit,
    shared_gate,
    shared_up,
    shared_down,
    routed_gate_weight,
    routed_up_weight,
    expert_down,
    route_ids,
    route_gates,
    piece_start,
    piece_length,
    block_grad,
):
    groups = lax.axis_size("ep")
    quarters = lax.axis_size("tp")
    me_ep = lax.axis_index("ep")
    me_tp = lax.axis_index("tp")
    count, width = tokens.shape
    part = count // quarters
    local_heads = query_weight.shape[1] // HD
    wide = local_heads * HD
    factor = HD ** (-0.5)

    def own(array):
        return lax.dynamic_slice_in_dim(array, me_tp * part, part, 0)

    dense = jnp.sum(
        own(route_gates)[:, :, None]
        * (own(route_ids)[:, :, None] == jnp.arange(groups, dtype=jnp.int32)).astype(F32),
        axis=1,
    )
    shard_rows = query_weight.shape[0]
    high = dense.astype(BF)
    low = (dense - high.astype(F32)).astype(BF)
    packed = jnp.concatenate([high.reshape(-1), low.reshape(-1)]).reshape(-1, shard_rows)
    spare = jnp.concatenate([jnp.stack([second_gain, shared_logit]), packed])
    spare = jnp.pad(spare, ((0, -spare.shape[0] % 16), (0, 0)))
    first = jnp.pad(first_gain[:, None], ((0, 0), (0, 127)))
    projection = jnp.concatenate([query_weight, key_weight, value_weight, first], axis=1)

    routed_gate, routed_up, routed_down = lax.optimization_barrier(
        (routed_gate_weight[0], routed_up_weight[0], expert_down[0], projection)
    )[:3]
    own_units = jnp.stack([routed_gate.T, routed_up.T, routed_down])
    rows = own_units.shape[1]
    routed = quarters * rows
    units_dev = shared_down.shape[0]
    piece = units_dev // groups
    x_units = swap_tp(own_units, 2)
    core_units = swap_tp(own_units, 1)

    def near_units(block):
        own_part, units = lax.optimization_barrier(
            (own_units, jnp.zeros((3, routed + quarters * piece, width), BF), block)
        )[:2]
        return place(units, [(0, own_part), (2, core_units)], 0)

    def nothing(block):
        return ()

    qkv_blocks, done = gather_ep(projection, [nothing, nothing, near_units])
    units = done[2]
    first = stack_absolute([block[:, 3 * wide :] for block in qkv_blocks])
    gain_one32 = first[:, :, 0].reshape(1, width).astype(F32)
    w_qkv = stack_absolute([block[:, : 3 * wide] for block in qkv_blocks]).reshape(width, -1)

    inputs32 = tokens.astype(F32)
    scale_one = rms_scale(inputs32)
    act1 = (inputs32 * scale_one * gain_one32).astype(BF)
    positions = jnp.arange(count, dtype=jnp.int32)
    start = piece_start[0]
    inside = (positions >= start) & (positions < start + piece_length[0])
    visible = (positions[None, :] <= positions[:, None]) | inside[:, None] & inside[None, :]
    all_lse, mixes, projected = [], [], []

    def project(block):
        projected.append(nn(after(act1, block), w_qkv).astype(BF))
        return projected[0]

    def attend(heads):
        def run(block):
            done = []
            for h in heads:
                query_h = after(columns(projected[0], h), block)
                key_h = columns(projected[0], local_heads + h)
                value_h = columns(projected[0], 2 * local_heads + h)
                scores = jnp.where(visible, nt(query_h, key_h) * factor, -1e30)
                highest = jnp.max(scores, axis=-1, keepdims=True)
                total = jnp.sum(jnp.exp(scores - highest), axis=-1, keepdims=True)
                all_lse.append(highest + jnp.log(total))
                probs = jnp.exp(scores - all_lse[h]).astype(BF)
                mixes.append(nn(probs, value_h).astype(BF))
                done += [all_lse[h], mixes[h]]
            return done

        return run

    half = local_heads // 2

    shared = jnp.stack([shared_gate.T, shared_up.T, shared_down]).reshape(3, groups, piece, -1)
    shared = lax.all_to_all(
        after(shared, qkv_blocks[-1]), "ep", split_axis=1, concat_axis=1, tiled=True
    )

    def attend_last(block):
        done = attend(range(half, local_heads))(block)
        return done, after(shared.transpose(0, 2, 1, 3).reshape(3, piece, width), block)

    blocks, done = gather_ep(
        after(jnp.concatenate([output_weight, spare]), qkv_blocks[-1]),
        [project, attend(range(half)), attend_last],
    )
    shared = done[2][1]
    x_shared = swap_tp(shared, 2)
    qkv = projected[0]
    query, key, value = qkv[:, :wide], qkv[:, wide : 2 * wide], qkv[:, 2 * wide :]
    spare = stack_absolute([block[wide:] for block in blocks])
    w_out = stack_absolute([block[:wide] for block in blocks])
    w_out = w_out.transpose(0, 2, 1).reshape(width, wide)
    gain_two32 = spare[:, 0].reshape(1, width).astype(F32)
    logit32 = spare[:, 1].reshape(1, width).astype(F32)
    packed = spare[:, 2 : 2 + packed.shape[0]]
    packed = packed.reshape(groups, 2, part, groups).astype(F32).sum(axis=1)
    chosen = jnp.arange(groups, dtype=jnp.int32)
    gates = jnp.sum(jnp.where(chosen == me_ep, packed, 0.0), axis=2)
    order = jnp.stack(relative_to_absolute())
    gates = jnp.sum(jnp.where((order[:, None] == chosen)[:, :, None], gates[None], 0.0), axis=1)
    gates = gates.reshape(groups * part, 1)

    attn_mix = jnp.concatenate(mixes, axis=1)
    branch = nt(attn_mix, w_out).reshape(quarters, part, width)
    attn_branch = scatter_tp_rows(branch)
    inputs_own = own(tokens).astype(F32)
    resid = inputs_own + attn_branch
    scale_two = rms_scale(resid)
    act2 = (resid * scale_two * gain_two32).astype(BF)

    def far_units(block):
        x_part = after(x_units, block)
        return place(units, [(1, x_part), (3, swap_tp(x_part, 1))], 0)

    def shared_units(block):
        x_part = after(x_shared, block)
        return [(0, shared), (1, x_part), (2, swap_tp(shared, 1)), (3, swap_tp(x_part, 1))]

    act_blocks, done = gather_ep(act2, [far_units])
    units = place(done[0], shared_units(act_blocks[-1]), routed)
    act_all = stack_static(act_blocks).reshape(groups * part, width)
    gout_own = after(own(block_grad), act_blocks[-2])

    def tokens_back(block):
        return block.reshape(groups, part, width)

    def prepare_shared(total):
        total = total.astype(BF).reshape(3, piece, groups, -1).transpose(0, 2, 1, 3)
        return lax.optimization_barrier(total)

    steps = -(-groups * part // 768)
    if steps == 1:
        score = score_of(act_all, logit32)
        coef = unit_coefs(gates, score, units, routed)

        def forward_gate(token):
            return nt(after(act_all, token), units[0])

        kept = []

        def forward_up(token):
            up_val = nt(after(act_all, token), units[1])
            hidden = (jax.nn.silu(kept[0]) * up_val * coef).astype(BF)
            return up_val, hidden

        def output(token):
            return nn(after(kept[2], token), units[2]).astype(BF)

        def keep_up(token):
            kept.extend(forward_up(token))
            return kept[1:]

        def keep_gate(token):
            kept.append(forward_gate(token))
            return kept[0]

        blocks, done = gather_ep(
            gout_own, [keep_gate, keep_up, output]
        )
        gate_val = done[0]
        up_val, hidden = done[1]
        ffn_part = done[2]
        gout_all = stack_static(blocks).reshape(groups * part, width)
        ffn_part = tokens_back(ffn_part)
        back = {}

        def backward(token):
            back["grads"], back["gscore"] = expert_back(
                gout_all, coef, score, (gate_val, up_val), units, routed
            )
            return back["grads"], back["gscore"]

        def rows_gate(token):
            back["rows"] = nn(after(back["grads"][0], token), units[0])
            return back["rows"]

        def rows_up(token):
            total = back["rows"] + nn(after(back["grads"][1], token), units[1])
            return (total + back["gscore"] * logit32).astype(BF)

        state = {"sum": [], "got": [], "x": None}

        def weight_grad(j, token, first, last):
            left = (hidden if j == 2 else back["grads"][j])[:, first:last]
            return tn(left, after(gout_all if j == 2 else act_all, token)).astype(BF)

        def shared_work(token):
            full = jnp.stack([weight_grad(j, token, routed, None) for j in range(3)])
            state["shared"] = full
            away = full[:, 2 * piece :]
            state["shared_got"] = swap_tp(away, 1)
            return away

        def routed_grad(j, token):
            full = weight_grad(j, token, 0, routed)
            away = full[2 * rows :]
            state["sum"].append(full)
            state["got"].append(swap_tp(away, 1))
            return full, away

        def shared_sum(index):
            span = slice(index * piece, (index + 1) * piece)
            return state["shared"][:, span].astype(F32) + state["shared_got"][:, span].astype(F32)

        def summed(j, index):
            span = slice(index * rows, (index + 1) * rows)
            return state["sum"][j][span].astype(F32) + state["got"][j][span].astype(F32)

        def routed_ready(js, token):
            along_x = jnp.concatenate([summed(j, 1) for j in js]).astype(BF)
            state["ready"] = after(along_x, token)
            return state["ready"]

        def routed_x(js, token):
            if "ready" not in state:
                routed_ready(js, token)
            along_x = after(state.pop("ready"), token)
            arrived = swap_tp(along_x, 2)
            state["x"] = arrived if state["x"] is None else jnp.concatenate([state["x"], arrived])
            return along_x

        def gate_work(token):
            along_x = after(shared_sum(1).astype(BF), token)
            state["shared_x"] = swap_tp(along_x, 2)
            return routed_grad(0, token), along_x

        def up_work(token):
            state["logit"] = jnp.sum(after(act_all, token).astype(F32) * back["gscore"], axis=0)
            return routed_grad(1, token), state["logit"]

        def last_work(token):
            return routed_grad(2, token)

        def total_work(token):
            state["total"] = prepare_shared(shared_sum(0) + state["shared_x"].astype(F32))
            return state["total"]

        ffn_branch, done = scatter_ep(
            lambda r: ffn_part[r], [backward, rows_gate, rows_up, shared_work]
        )
        gact_part = tokens_back(done[2])
        gact2, _ = scatter_ep(lambda r: gact_part[r], [gate_work, up_work, nothing, total_work])
        logit_part = state["logit"]

        def shared_total():
            return state["total"]

        def expert_grads():
            arrived = state["x"].reshape(3, rows, width).astype(F32)
            return [summed(j, 0) + arrived[j] for j in range(3)]

    else:
        gout_all = stack_static(gather_ep(gout_own)).reshape(groups * part, width)
        ffn_part, gact_part, logit_part, sums = experts_in_blocks(
            act_all, gout_all, gates, logit32, units, routed, steps
        )
        ffn_part, gact_part = tokens_back(ffn_part), tokens_back(gact_part)
        gact2 = scatter_ep(lambda r: gact_part[r])
        ffn_branch = scatter_ep(lambda r: ffn_part[r])

        def relative(j, first, last):
            parts = sums[j][first:last].reshape(2, 2, -1, width)
            return scatter_tp(parts.astype(BF))

        def last_work(token):
            return ()

        def routed_ready(js, token):
            return ()

        def routed_x(js, token):
            return ()

        def expert_grads():
            return [relative(j, 0, routed) for j in range(3)]

        def shared_total():
            return prepare_shared(jnp.stack([relative(j, routed, None) for j in range(3)]))

    block_sum = resid + ffn_branch
    squares = jnp.stack(
        [
            jnp.sum(attn_branch * attn_branch),
            jnp.sum(ffn_branch * ffn_branch),
            jnp.sum(block_sum * block_sum),
        ]
    )

    resid_part, gain_two_part = norm_back(gact2, resid, scale_two, gain_two32)
    gresid = own(block_grad).astype(F32) + resid_part
    tail = {"shared": shared_total()}
    gresid = after(gresid, tail["shared"])
    gattn = after(gather_tp_rows(gresid.astype(BF)), *jax.tree.leaves(last_work(gresid)))
    block_out = gather_tp_rows(after(block_sum.astype(BF), gattn))
    vectors = jnp.stack([gain_two_part, logit_part], axis=1).reshape(groups, -1, 2)
    vectors = jnp.pad(vectors, ((0, 0), (0, 0), (0, 126))).astype(BF)
    out_grads = tn(gattn, attn_mix).astype(BF).reshape(groups, -1, wide)
    gmix = nn(gattn, w_out).astype(BF)

    def head_back(h):
        def run(token):
            gmix_h = columns(gmix, h)
            if token is not None:
                gmix_h = after(gmix_h, token)
            query_h, key_h = columns(query, h), columns(key, h)
            scores = jnp.where(visible, nt(query_h, key_h) * factor, -1e30)
            probs = jnp.exp(scores - all_lse[h])
            gprob = nt(gmix_h, columns(value, h))
            gvalue = tn(probs.astype(BF), gmix_h).astype(BF)
            inner = jnp.sum(probs * gprob, axis=-1, keepdims=True)
            gscores = (probs * (gprob - inner)).astype(BF)
            gquery = (nn(gscores, key_h) * factor).astype(BF)
            gkey = (tn(gscores, query_h) * factor).astype(BF)
            return gquery, gkey, gvalue

        return run

    def heads_back(first, last):
        def run(token):
            sent = routed_x([0], gattn) if first == 0 else (routed_x([1], token), routed_ready([2], token))
            if first == 0:
                tail["squares"] = sum_tp(after(squares, gattn))
            return [head_back(h)(token) for h in range(first, last)], sent

        return run

    out_grads, heads = scatter_absolute(
        jnp.concatenate([out_grads, vectors], axis=2), [heads_back(0, half), heads_back(half, local_heads)]
    )
    heads = heads[0][0] + heads[1][0]
    output_grad = out_grads[:, :wide].T
    early = sum_tp(out_grads[:, wide : wide + 2])
    gqkv = jnp.concatenate([head[i] for i in range(3) for head in heads], axis=1)
    gqkv_grad = tn(act1, gqkv).astype(BF).reshape(groups, -1, 3 * wide)

    def gact1_work(token):
        shared = lax.all_to_all(tail["shared"], "ep", split_axis=1, concat_axis=1, tiled=True)
        gact1 = nt(after(gqkv, gqkv_grad), w_qkv).astype(BF).reshape(quarters, part, width)
        tail["gact1"] = scatter_tp_rows_start(gact1)
        return gact1, shared

    def tokens_work(token):
        gact1 = sum(part.astype(F32) for part in after(tail["gact1"], token))
        input_part, _ = norm_back(gact1, inputs_own, own(scale_one), gain_one32)
        tail["tokens"] = (gresid + input_part).astype(BF)
        return tail["tokens"], routed_x([2], gact1)

    qkv_grad, done = scatter_absolute(
        gqkv_grad, [gact1_work, tokens_work]
    )
    shared_grads, squares = done[0][1], tail["squares"]
    rms_values = jnp.sqrt(squares / (count * width))[None, :]
    tokens_grad = gather_tp_rows(tail["tokens"]).astype(F32)

    shared_grads = shared_grads.reshape(3, units_dev, -1)
    sgate_grad = shared_grads[0].T.astype(F32)
    sup_grad = shared_grads[1].T.astype(F32)
    sdown_grad = shared_grads[2].astype(F32)
    gate_grad, up_grad, down_grad = expert_grads()

    own_qkv = jnp.concatenate([query_weight, key_weight, value_weight], axis=1).astype(F32)
    late = sum_tp(jnp.sum(own_qkv * qkv_grad, axis=1) / first_gain.astype(F32))
    return (
        block_out,
        tokens_grad,
        late,
        qkv_grad[:, :wide],
        qkv_grad[:, wide : 2 * wide],
        qkv_grad[:, 2 * wide :],
        output_grad,
        early[:, 0],
        early[:, 1],
        sgate_grad,
        sup_grad,
        sdown_grad,
        gate_grad.T[None],
        up_grad.T[None],
        down_grad[None],
        rms_values,
    )


def solution(mesh):
    in_specs = (
        P("ep", None),
        P("ep"),
        P("ep", "tp"),
        P("ep", "tp"),
        P("ep", "tp"),
        P("tp", "ep"),
        P("ep"),
        P("ep"),
        P("ep", "tp"),
        P("ep", "tp"),
        P("tp", "ep"),
        P("ep", None, "tp"),
        P("ep", None, "tp"),
        P("ep", "tp", None),
        P("ep", None),
        P("ep", None),
        P("ep"),
        P("ep"),
        P("ep", None),
    )
    out_specs = (
        P("ep", None),
        P("ep", None),
        P("ep"),
        P("ep", "tp"),
        P("ep", "tp"),
        P("ep", "tp"),
        P("tp", "ep"),
        P("ep"),
        P("ep"),
        P("ep", "tp"),
        P("ep", "tp"),
        P("tp", "ep"),
        P("ep", None, "tp"),
        P("ep", None, "tp"),
        P("ep", "tp", None),
        P("ep", None),
    )
    return jax.shard_map(
        on_device, mesh=mesh, in_specs=in_specs, out_specs=out_specs, check_vma=False
    )
```
